32 devices in a mesh: group: 4 (over z), depth: 2 (over x), image: 4 (over y, core).
Axes of the slice: x: 2, y: 2, z: 4, core: 2. Of those that a mesh axis runs over, the one named last changes fastest.
Arguments:
- density: float32 [16, 192, 512], P('depth', 'group', 'image'), may hold values from 0.5 to 1.5
- velocity: float32 [3, 16, 192, 512], P(None, 'depth', 'group', 'image'), may hold values from -1.2 to 1.2
- pressure: float32 [16, 192, 512], P('depth', 'group', 'image'), may hold values from 0.5 to 1.5
- palette: float32 [4, 256], replicated, may hold values from 0.2 to 2
- palette_index: int32 [8, 256], replicated, may hold values from 0 to 255
Outputs:
- fluid_state: float32 [5, 16, 192, 512], P(None, 'depth', 'group', 'image')
- picture: float32 [8, 3, 192, 512], P('depth', None, 'group', 'image')
The draws below stay inside these ranges and needn't reach their ends.
All inputs are finite; a program needn't handle non-finite values.
Results may differ from the reference program's by a relative error of at most 0.0003.
Values sent between devices are 32-bit elements; how exact they have to be, the bound alone decides.
No kernel may reach another device: no remote copies, remote signals or barrier semaphores. Data moves between devices by JAX's collectives and lax.ppermute only.
A program may use at most 128 MiB of HBM per device.

```python
import math
import jax
import jax.numpy as jnp
from jax import lax

NTF = 8
BINS = 256
PALETTE = 256
CX = 64
NX = 192
NY = 512
NZ = 16


def set_ends(drawn, own_key, least, largest):
    index_at = [jax.random.randint(jax.random.fold_in(own_key, axis), (), 0, length) for axis, length in enumerate(drawn.shape)]
    widest = drawn.shape.index(max(drawn.shape))
    neighbour = index_at[:widest] + [(index_at[widest] + 1) % drawn.shape[widest]] + index_at[widest + 1:]
    return drawn.at[tuple(index_at)].set(least).at[tuple(neighbour)].set(largest)


def steps_of(key, extent, shards, smallest, high):
    def one(axis_at, shards_of):
        heights = jax.random.uniform(jax.random.fold_in(jax.random.fold_in(key, 6), axis_at), (shards_of,), jnp.float32, smallest / len(shards), high / len(shards))
        return jnp.repeat(jnp.exp(heights), extent[axis_at] // shards_of).reshape((-1,) + (1,) * (len(extent) - axis_at - 1))

    gain = one(*shards[0])
    for cut in shards[1:]:
        gain = gain * one(*cut)
    return gain


def noise(own_key, shape, deviation, reach, cuts=(), kind=jnp.bfloat16):
    values = jax.random.normal(own_key, shape, jnp.float32) * deviation
    if len(cuts) > 0:
        values = steps_of(own_key, shape, cuts, -0.22, 0.18) * values
    return jnp.clip(values, min=-reach, max=reach).astype(kind)


def setup_inputs(seed: int = 0) -> dict:
    key_of = jax.random.split(jax.random.key(seed), 6)
    density = jnp.clip(0.5 + 1.0 * jax.random.uniform(key_of[0], (NZ, NX, NY), jnp.float32) ** steps_of(key_of[0], (NZ, NX, NY), ((0, 2), (1, 4), (2, 4)), -0.2, 0.2), 0.5, 1.5)
    velocity = noise(key_of[1], (3, NZ, NX, NY), 0.3, 1.2, ((1, 2), (2, 4), (3, 4)), jnp.float32)
    pressure = jnp.clip(0.5 + 1.0 * jax.random.uniform(key_of[2], (NZ, NX, NY), jnp.float32) ** steps_of(key_of[2], (NZ, NX, NY), ((0, 2), (1, 4), (2, 4)), -0.2, 0.2), 0.5, 1.5)
    palette = jnp.clip(jnp.exp(jax.random.uniform(key_of[3], (4, PALETTE), jnp.float32, math.log(0.2), math.log(2.0))), 0.2, 2.0)
    palette_index = set_ends(jax.random.randint(key_of[4], (NTF, BINS), 0, PALETTE), jax.random.fold_in(key_of[4], 1), 0, PALETTE - 1).astype(jnp.int32)
    return {"density": density, "velocity": velocity, "pressure": pressure, "palette": palette, "palette_index": palette_index}


HEAT_RATIO = 1.4
COURANT = 0.8

def leading(values, direction):
    return lax.slice_in_dim(values, 0, values.shape[direction] - 1, axis=direction)

def trailing(values, direction):
    return lax.slice_in_dim(values, 1, values.shape[direction], axis=direction)

def conserved(density, velocity, pressure):
    momentum = density[None] * velocity
    kinetic = 0.5 * density * lax.optimization_barrier(jnp.sum(velocity * velocity, axis=0))
    return jnp.concatenate([density[None], momentum, (pressure / (HEAT_RATIO - 1.0) + kinetic)[None]], axis=0)

def primitives(fluid_state):
    density = fluid_state[0]
    velocities = fluid_state[1:4] / density[None]
    kinetic = 0.5 * lax.optimization_barrier(jnp.sum(fluid_state[1:4] * velocities, axis=0))
    pressures = (HEAT_RATIO - 1.0) * (fluid_state[4] - kinetic)
    return (density, velocities, pressures)

def euler_flux(fluid_state, component):
    density, velocities, pressures = primitives(fluid_state)
    normal = velocities[component - 1]
    rows = [fluid_state[0] * normal, fluid_state[1] * normal, fluid_state[2] * normal, fluid_state[3] * normal, (fluid_state[4] + pressures) * normal]
    rows[component] = rows[component] + pressures
    signal = jnp.abs(normal) + jnp.sqrt(HEAT_RATIO * pressures / density)
    return (jnp.stack(rows), signal)

def tendency(padded):
    summed = None
    for direction, component in ((1, 3), (2, 1), (3, 2)):
        strip_cells = padded
        for across in (1, 2, 3):
            if across != direction:
                strip_cells = lax.slice_in_dim(strip_cells, 1, strip_cells.shape[across] - 1, axis=across)
        fluxes, signal = euler_flux(strip_cells, component)
        fastest_face = jnp.maximum(leading(signal, direction - 1), trailing(signal, direction - 1))
        face_flux = 0.5 * (leading(fluxes, direction) + trailing(fluxes, direction)) - 0.5 * fastest_face[None] * (trailing(strip_cells, direction) - leading(strip_cells, direction))
        change = trailing(face_flux, direction) - leading(face_flux, direction)
        summed = change if summed is None else summed + change
    return -summed

def wave_bound(fluid_state):
    density, velocities, pressures = primitives(fluid_state)
    return jnp.max(lax.optimization_barrier(jnp.sum(jnp.abs(velocities), axis=0)) + 3.0 * jnp.sqrt(HEAT_RATIO * pressures / density))

def mirror_sign():
    return jnp.array([1.0, -1.0, 1.0, 1.0, 1.0], jnp.float32)[:, None, None, None]

def colour_table(palette, palette_index):
    count_tf = palette_index.shape[0]
    count_bins = palette_index.shape[1]
    onehot = (jnp.arange(palette.shape[1], dtype=jnp.int32)[:, None] == palette_index.reshape(-1)[None, :]).astype(jnp.float32)
    table = jnp.dot(palette, onehot, precision=lax.Precision.HIGHEST)
    return table.reshape(4, count_tf, count_bins).transpose(1, 0, 2).reshape(count_tf * 4, count_bins)

def sheet_shares(screen_shades, unrolled_mass_per_volume, thermal_grid_quantity, ray_increment_distance):
    count_bins = screen_shades.shape[1]
    position = jnp.clip(unrolled_mass_per_volume - 0.5, 0.0, 1.0) * (count_bins - 1)
    hat_weights = jnp.maximum(0.0, 1.0 - jnp.abs(position[None, :] - jnp.arange(count_bins, dtype=jnp.float32)[:, None]))
    shade_mapping_index = jnp.dot(screen_shades, hat_weights, precision=lax.Precision.HIGHEST).reshape(screen_shades.shape[0] // 4, 4, unrolled_mass_per_volume.shape[0])
    extinct = shade_mapping_index[:, 3] * unrolled_mass_per_volume[None] * ray_increment_distance
    absorbance_entries = 1.0 - jnp.exp(-extinct)
    radiance_source = shade_mapping_index[:, :3] * (absorbance_entries * thermal_grid_quantity[None])[:, None]
    return (extinct, radiance_source)

def march_slab(screen_shades, density_field, heat_field, ray_increment_distance):
    count_tf = screen_shades.shape[0] // 4
    planes = density_field.shape[0]
    cell_count = density_field.shape[1] * density_field.shape[2]

    def march_plane(carried, slab):
        optical, colour = carried
        extinct, radiance_source = sheet_shares(screen_shades, slab[0], slab[1], ray_increment_distance)
        return ((optical + extinct, colour + jnp.exp(-optical)[:, None] * radiance_source), None)
    initial = (jnp.zeros((count_tf, cell_count), jnp.float32), jnp.zeros((count_tf, 3, cell_count), jnp.float32))
    (optical, colour), unused = lax.scan(march_plane, initial, (density_field.reshape(planes, cell_count), heat_field.reshape(planes, cell_count)))
    return (optical, colour)

def reference(density, velocity, pressure, palette, palette_index):
    initial_state = conserved(density, velocity, pressure)
    time_step = COURANT / wave_bound(initial_state)

    def full_tendency(values):
        walled = jnp.concatenate([values[:, :, :1] * mirror_sign(), values, values[:, :, -1:] * mirror_sign()], axis=2)
        padded = jnp.pad(walled, ((0, 0), (1, 1), (0, 0), (1, 1)), mode='wrap')

        def block_tendency(block):
            return tendency(lax.dynamic_slice_in_dim(padded, block * CX, CX + 2, axis=2))
        pieces = lax.map(block_tendency, jnp.arange(NX // CX, dtype=jnp.int32))
        return jnp.moveaxis(pieces, 0, 2).reshape(values.shape)
    section_one = initial_state + time_step * full_tendency(initial_state)
    section_two = 0.75 * initial_state + 0.25 * (section_one + time_step * full_tendency(section_one))
    section_three = initial_state / 3.0 + 2.0 / 3.0 * (section_two + time_step * full_tendency(section_two))
    screen_shades = colour_table(palette, palette_index)
    field_density, velocities, pressures = primitives(section_three)
    optical, colour = march_slab(screen_shades, field_density, pressures / field_density, 2.0 / NZ)
    return (section_three, colour.reshape(NTF, 3, NX, NY))
```

```python
import jax
import jax.numpy as jnp
from jax import lax
from jax.experimental import pallas as pl
from jax.experimental.pallas import tpu as pltpu
from jax.sharding import PartitionSpec as P

HEAT_RATIO = 1.4
COURANT = 0.8


def extended(array, sides, width, wrap):
    for axis, dim in sides:
        size, length = (lax.axis_size(axis), array.shape[dim])
        up = [(i, (i + 1) % size) for i in range(size if wrap else size - 1)]
        down = [(j, i) for i, j in up]
        last = lax.slice_in_dim(array, length - width, length, axis=dim)
        first = lax.slice_in_dim(array, 0, width, axis=dim)
        before = lax.ppermute(last, axis, up)
        after = lax.ppermute(first, axis, down)
        array = jnp.concatenate([before, array, after], axis=dim)
    return array


def leading(values, direction):
    return lax.slice_in_dim(values, 0, values.shape[direction] - 1, axis=direction)


def trailing(values, direction):
    return lax.slice_in_dim(values, 1, values.shape[direction], axis=direction)


def conserved(density, velocity, pressure):
    momentum = density[None] * velocity
    kinetic = 0.5 * density * jnp.sum(velocity * velocity, axis=0)
    return jnp.concatenate(
        [density[None], momentum, (pressure / (HEAT_RATIO - 1.0) + kinetic)[None]], axis=0
    )


def primitives(fluid_state):
    density = fluid_state[0]
    velocities = fluid_state[1:4] / density[None]
    kinetic = 0.5 * jnp.sum(fluid_state[1:4] * velocities, axis=0)
    pressures = (HEAT_RATIO - 1.0) * (fluid_state[4] - kinetic)
    return (density, velocities, pressures)


def euler_flux(fluid_state, component):
    density, velocities, pressures = primitives(fluid_state)
    normal = velocities[component - 1]
    rows = [
        fluid_state[0] * normal,
        fluid_state[1] * normal,
        fluid_state[2] * normal,
        fluid_state[3] * normal,
        (fluid_state[4] + pressures) * normal,
    ]
    rows[component] = rows[component] + pressures
    signal = jnp.abs(normal) + jnp.sqrt(HEAT_RATIO * pressures / density)
    return (jnp.stack(rows), signal)


def tendency(padded):
    summed = None
    for direction, component in ((1, 3), (2, 1), (3, 2)):
        strip_cells = padded
        for across in (1, 2, 3):
            if across != direction:
                strip_cells = lax.slice_in_dim(
                    strip_cells, 1, strip_cells.shape[across] - 1, axis=across
                )
        fluxes, signal = euler_flux(strip_cells, component)
        fastest_face = jnp.maximum(leading(signal, direction - 1), trailing(signal, direction - 1))
        face_flux = 0.5 * (
            leading(fluxes, direction) + trailing(fluxes, direction)
        ) - 0.5 * fastest_face[None] * (
            trailing(strip_cells, direction) - leading(strip_cells, direction)
        )
        change = trailing(face_flux, direction) - leading(face_flux, direction)
        summed = change if summed is None else summed + change
    return -summed


def wave_bound(fluid_state):
    density, velocities, pressures = primitives(fluid_state)
    return jnp.max(
        jnp.sum(jnp.abs(velocities), axis=0) + 3.0 * jnp.sqrt(HEAT_RATIO * pressures / density)
    )


def lanes(values, index):
    return jnp.take_along_axis(values, index, axis=1)

def render_kernel(scale, rho_ref, heat_ref, palette_ref, index_ref, out_ref, table, ke, ko, we, wo):
    planes, rows, width = rho_ref.shape
    count_tf, bins = index_ref.shape
    half = bins // 2
    lane = lax.broadcasted_iota(jnp.int32, (count_tf, half), 1)
    low, high = index_ref[:, :half], index_ref[:, half:]
    for parity in range(2):
        at = lane * 2 + parity
        inside = jnp.where(at < half, at, at - half)
        colour = jnp.where(at < half, lanes(low, inside), lanes(high, inside))
        wrapped = jnp.where(colour < half, colour, colour - half)
        for c in range(4):
            first = jnp.broadcast_to(palette_ref[c:c+1, :half], (count_tf, half))
            second = jnp.broadcast_to(palette_ref[c:c+1, half:], (count_tf, half))
            table[c, parity] = jnp.where(colour < half, lanes(first, wrapped), lanes(second, wrapped))
    def prepare(z, _):
        position = jnp.clip(rho_ref[z] - 0.5, 0.0, 1.0) * (bins - 1)
        cell = jnp.minimum(position.astype(jnp.int32), bins - 2)
        even = (cell + 1) >> 1
        odd = cell >> 1
        ke[z] = even
        ko[z] = odd
        we[z] = 1.0 - jnp.abs(position - (2 * even).astype(jnp.float32))
        wo[z] = 1.0 - jnp.abs(position - (2 * odd + 1).astype(jnp.float32))
        return 0
    lax.fori_loop(0, planes, prepare, 0)
    tables = [[table[c, p] for p in range(2)] for c in range(4)]
    def ray(x, _):
        trans = jnp.ones((count_tf, width), jnp.float32)
        light = [jnp.zeros((count_tf, width), jnp.float32) for _ in range(3)]
        for z in range(planes):
            def wide(ref):
                return jnp.broadcast_to(ref[z, pl.ds(x, 1), :], (count_tf, width))
            ie, io, fe, fo = wide(ke), wide(ko), wide(we), wide(wo)
            looked = [lanes(tables[c][0], ie) * fe + lanes(tables[c][1], io) * fo for c in range(4)]
            passed = jnp.exp(looked[3] * (wide(rho_ref) * -scale))
            weight = trans * (1.0 - passed) * wide(heat_ref)
            light = [light[c] + looked[c] * weight for c in range(3)]
            trans = trans * passed
        for c, values in enumerate(light + [trans]):
            out_ref[pl.ds(c * rows + x, count_tf, stride=4 * rows), :] = values
        return 0
    lax.fori_loop(0, rows, ray, 0)

def render(rho, heat, palette, index, scale):
    planes, rows, width = rho.shape
    count_tf, bins = index.shape
    out = pl.pallas_call(
        lambda *refs: render_kernel(scale, *refs),
        out_shape=jax.ShapeDtypeStruct((count_tf * 4 * rows, width), jnp.float32),
        in_specs=[pl.BlockSpec(memory_space=pltpu.VMEM)] * 4,
        out_specs=pl.BlockSpec(memory_space=pltpu.VMEM),
        scratch_shapes=[pltpu.VMEM((4, 2, count_tf, bins // 2), jnp.float32)]
        + [pltpu.VMEM((planes, rows, width), jnp.int32)] * 2
        + [pltpu.VMEM((planes, rows, width), jnp.float32)] * 2,
        name="render",
    )(rho, heat, palette, index)
    return out.reshape(count_tf, 4, rows, width)


def largest(value, axes):
    for axis in axes:
        size = lax.axis_size(axis)
        step = 1
        while step < size:
            route = [(i, (i + step) % size) for i in range(size)]
            value = jnp.maximum(value, lax.ppermute(value, axis, route))
            step *= 2
    return value


def mirror_sign():
    return jnp.array([1.0, -1.0, 1.0, 1.0, 1.0], jnp.float32)[:, None, None, None]


def widen(values):
    row_index, rows = lax.axis_index("group"), lax.axis_size("group")
    sided = extended(values, (("group", 2),), 1, False)
    lower = jnp.where(row_index == 0, values[:, :, :1] * mirror_sign(), sided[:, :, :1])
    upper = jnp.where(row_index == rows - 1, values[:, :, -1:] * mirror_sign(), sided[:, :, -1:])
    walled = jnp.concatenate([lower, values, upper], axis=2)
    return extended(walled, (("depth", 1), ("image", 3)), 1, True)


def composed(shares):
    light, passed = None, None
    for d in range(shares.shape[0]):
        slab = shares[d]
        light = slab[:, :3] if d == 0 else light + passed * slab[:, :3]
        passed = slab[:, 3:] if d == 0 else passed * slab[:, 3:]
    return light


def exchanged(shares):
    depth = lax.axis_size("depth")
    count_tf = shares.shape[0]
    per_dev = count_tf // depth
    parts = shares.reshape((depth, per_dev) + shares.shape[1:])
    if depth == 2:
        me = lax.axis_index("depth")
        mine = jnp.where(me == 0, parts[0], parts[1])
        other = lax.ppermute(jnp.where(me == 0, parts[1], parts[0]), "depth", [(0, 1), (1, 0)])
        front = jnp.where(me == 0, mine, other)
        back = jnp.where(me == 0, other, mine)
        return front[:, :3] + front[:, 3:] * back[:, :3]
    return composed(lax.all_to_all(parts, "depth", 0, 0, tiled=True))


def shards(density, velocity, pressure, palette, palette_index):
    initial_state = conserved(density, velocity, pressure)
    fastest = largest(wave_bound(initial_state)[None], ("image", "depth", "group"))[0]
    time_step = COURANT / fastest

    def change(values):
        return tendency(widen(values))

    section_one = initial_state + time_step * change(initial_state)
    section_two = 0.75 * initial_state + 0.25 * (section_one + time_step * change(section_one))
    fluid_state = initial_state / 3.0 + 2.0 / 3.0 * (
        section_two + time_step * change(section_two)
    )
    field_density, velocities, pressures = primitives(fluid_state)
    planes = density.shape[0] * lax.axis_size("depth")
    shares = render(field_density, pressures / field_density, palette, palette_index, 2.0 / planes)
    return (fluid_state, exchanged(shares))


def solution(mesh):
    return jax.shard_map(
        shards,
        mesh=mesh,
        in_specs=(
            P("depth", "group", "image"),
            P(None, "depth", "group", "image"),
            P("depth", "group", "image"),
            P(),
            P(),
        ),
        out_specs=(P(None, "depth", "group", "image"), P("depth", None, "group", "image")),
        check_vma=False,
    )
```

```python
import functools

import jax
import jax.numpy as jnp
from jax import lax
from jax.experimental import pallas as pl
from jax.experimental.pallas import tpu as pltpu
from jax.sharding import PartitionSpec as P

HEAT_RATIO = 1.4
COURANT = 0.8
REACH = 3
WINDOW = 3 * REACH
SUB = 8
VMEM = pl.BlockSpec(memory_space=pltpu.VMEM)


def ahead(values, distance=1):
    return pltpu.roll(values, values.shape[-1] - distance, axis=values.ndim - 1)


def behind(values, distance=1):
    return pltpu.roll(values, distance, axis=values.ndim - 1)


def turned(values, shift):
    return pltpu.roll(values, shift % values.shape[-1], axis=values.ndim - 1)


def padded_rows(rows):
    return -(-(rows + 2 * REACH) // SUB) * SUB


def primitives(rho, mx, my, mz, energy):
    inverse = 1.0 / rho
    ux, uy, uz = mx * inverse, my * inverse, mz * inverse
    pressure = (HEAT_RATIO - 1.0) * (energy - 0.5 * (mx * ux + my * uy + mz * uz))
    sound = jnp.sqrt(HEAT_RATIO * pressure * inverse)
    return ux, uy, uz, pressure, sound


def fluxes(state, normal, pressure, component):
    rho, mx, my, mz, energy = state
    rows = [state[component], mx * normal, my * normal, mz * normal, (energy + pressure) * normal]
    rows[component] = rows[component] + pressure
    return rows


def face(flux_a, flux_b, state_a, state_b, signal_a, signal_b):
    fastest = jnp.maximum(signal_a, signal_b)
    return [
        (fa + fb) - fastest * (ub - ua)
        for fa, fb, ua, ub in zip(flux_a, flux_b, state_a, state_b)
    ]


def opening_kernel(rho_ref, vel_ref, pre_ref, state_ref, zpay_ref, low_ref, high_ref, top_ref):
    planes, rows, width = rho_ref.shape
    edge = list(range(REACH)) + list(range(planes - REACH, planes))
    fastest = None
    for z in range(planes):
        rho, p = rho_ref[z], pre_ref[z]
        v = [vel_ref[i, z] for i in range(3)]
        signal = jnp.abs(v[0]) + jnp.abs(v[1]) + jnp.abs(v[2]) + 3.0 * jnp.sqrt(HEAT_RATIO * p / rho)
        signal = jnp.max(signal.reshape(rows // SUB, SUB, width), axis=0)
        fastest = signal if fastest is None else jnp.maximum(fastest, signal)
        kinetic = 0.5 * rho * (v[0] * v[0] + v[1] * v[1] + v[2] * v[2])
        fields = [rho, rho * v[0], rho * v[1], rho * v[2], p / (HEAT_RATIO - 1.0) + kinetic]
        for f in range(5):
            state_ref[f, z] = fields[f]
            if z in edge:
                zpay_ref[f, edge.index(z)] = fields[f]
            at = (f * planes + z) * REACH
            low_ref[at : at + REACH, :] = fields[f][:REACH]
            high_ref[at : at + REACH, :] = fields[f][rows - REACH :]
    top_ref[...] = fastest


def opening(density, velocity, pressure):
    planes, rows, width = density.shape
    f32 = jnp.float32
    return pl.pallas_call(
        opening_kernel,
        out_shape=[
            jax.ShapeDtypeStruct((5, planes, rows, width), f32),
            jax.ShapeDtypeStruct((5, 2 * REACH, rows, width), f32),
            jax.ShapeDtypeStruct((5 * planes * REACH, width), f32),
            jax.ShapeDtypeStruct((5 * planes * REACH, width), f32),
            jax.ShapeDtypeStruct((SUB, width), f32),
        ],
        in_specs=[VMEM] * 3,
        out_specs=[VMEM] * 5,
        name="opening",
    )(density, velocity, pressure)


def window_kernel(state_ref, low_ref, high_ref, wide_ref, right_ref, left_ref):
    planes, rows, width = state_ref.shape[1:]
    total = wide_ref.shape[2]
    group, groups = lax.axis_index("group"), lax.axis_size("group")
    lane = lax.broadcasted_iota(jnp.int32, (SUB, width), 1)
    for f in range(5):
        sign = -1.0 if f == 1 else 1.0
        for z in range(planes):
            at = (f * planes + z) * REACH
            wide_ref[f, z, REACH : REACH + rows, :] = state_ref[f, z]
            mirrored = [state_ref[f, z, r : r + 1, :] * sign for r in range(REACH - 1, -1, -1)]
            below = jnp.where(group == 0, jnp.concatenate(mirrored, axis=0), low_ref[at : at + REACH, :])
            wide_ref[f, z, :REACH, :] = below
            mirrored = [state_ref[f, z, rows - 1 - r : rows - r, :] * sign for r in range(REACH)]
            above = jnp.where(
                group == groups - 1, jnp.concatenate(mirrored, axis=0), high_ref[at : at + REACH, :]
            )
            wide_ref[f, z, REACH + rows : 2 * REACH + rows, :] = above

    def fields(f, carry):
        for t in range(total // SUB):
            cut = slice(SUB * t, SUB * (t + 1))
            right = jnp.zeros((SUB, width), jnp.float32)
            left = right
            for z in range(planes):
                start = WINDOW * (z + REACH)
                inside = (lane >= start) & (lane < start + WINDOW)
                values = wide_ref[f, z, cut, :]
                right = jnp.where(inside, turned(values, start - (width - 2 * REACH)), right)
                left = jnp.where(inside, turned(values, start - (width - REACH)), left)
            right_ref[f, cut, :] = right
            left_ref[f, cut, :] = left
        return carry

    lax.fori_loop(0, 5, fields, 0)


def windows(state, low, high):
    planes, rows, width = state.shape[1:]
    total = padded_rows(rows)
    f32 = jnp.float32
    return pl.pallas_call(
        window_kernel,
        out_shape=[
            jax.ShapeDtypeStruct((5, planes, total, width), f32),
            jax.ShapeDtypeStruct((5, total, width), f32),
            jax.ShapeDtypeStruct((5, total, width), f32),
        ],
        in_specs=[VMEM] * 3,
        out_specs=[VMEM] * 3,
        name="windows",
    )(state, low, high)


def strip_kernel(wide_ref, right_ref, left_ref, from_right, from_left, strips_ref, pay_ref):
    planes, total, width = wide_ref.shape[1:]
    rows = total - 2 * REACH - (total - 2 * REACH) % SUB
    lane = lax.broadcasted_iota(jnp.int32, (SUB, width), 1)
    column = lane % WINDOW
    span = WINDOW * REACH
    first, last = WINDOW * REACH, WINDOW * planes
    far = WINDOW * (REACH + planes)
    for f in range(5):
        for t in range(total // SUB):
            cut = slice(SUB * t, SUB * (t + 1))
            right = jnp.where(column >= 2 * REACH, from_right[f, cut, :], right_ref[f, cut, :])
            left = jnp.where(column < REACH, from_left[f, cut, :], left_ref[f, cut, :])
            strips_ref[0, f, cut, :] = left
            strips_ref[1, f, cut, :] = right
            sent = jnp.where(lane < span, turned(right, -last), left)
            pay_ref[f, cut, :] = jnp.where(lane >= far, turned(right, far - first), sent)
        low, high = REACH - 1, REACH + rows
        for side, (near, next_one) in enumerate(((0, 1), (planes - 1, planes - 2))):
            at = total + SUB * side
            pay_ref[f, at : at + 2, :] = wide_ref[f, near, low - 1 : low + 1, :]
            pay_ref[f, at + 2 : at + 3, :] = wide_ref[f, next_one, low : low + 1, :]
            pay_ref[f, at + 3 : at + 5, :] = wide_ref[f, near, high : high + 2, :]
            pay_ref[f, at + 5 : at + 6, :] = wide_ref[f, next_one, high : high + 1, :]
            pay_ref[f, at + 6 : at + 8, :] = jnp.zeros((2, width), jnp.float32)


def strips_of(wide, right, left, from_right, from_left):
    planes, total, width = wide.shape[1:]
    f32 = jnp.float32
    return pl.pallas_call(
        strip_kernel,
        out_shape=[
            jax.ShapeDtypeStruct((2, 5, total, width), f32),
            jax.ShapeDtypeStruct((5, total + 2 * SUB, width), f32),
        ],
        in_specs=[VMEM] * 5,
        out_specs=[VMEM] * 2,
        name="strips",
    )(wide, right, left, from_right, from_left)


def blend(section, base, here, change):
    if section == 0:
        return here + change
    if section == 1:
        return 0.75 * base + 0.25 * (here + change)
    return base * (1.0 / 3.0) + (2.0 / 3.0) * (here + change)


def section_kernel(shared, *refs):
    if shared:
        wide_ref, zone_ref, pay_ref, strips_ref, top_ref = refs[:5]
        zone_refs, pay_refs = (zone_ref, zone_ref), (pay_ref, pay_ref)
        rest = refs[5:]
    else:
        wide_ref, strips_ref, top_ref = refs[0], refs[5], refs[6]
        zone_refs, pay_refs = refs[1:3], refs[3:5]
        rest = refs[7:]
    out_ref, heat_ref, main, strip, fx, fz, fy, gz, gx, acc = rest
    planes, total, width = wide_ref.shape[1:]
    rows = out_ref.shape[2]
    tiles = total // SUB
    lane = lax.broadcasted_iota(jnp.int32, (SUB, width), 1)
    far = WINDOW * (REACH + planes)
    for f in range(5):
        for z in range(planes):
            main[0, f, z + REACH, :total, :] = wide_ref[f, z]
        for z in range(REACH):
            main[0, f, z, REACH : REACH + rows, :] = zone_refs[0][f, REACH + z]
            main[0, f, planes + REACH + z, REACH : REACH + rows, :] = zone_refs[1][f, z]
        low, high = REACH - 1, REACH + rows
        for pay, near, next_one, at in (
            (pay_refs[1], planes + REACH, planes + REACH + 1, total),
            (pay_refs[0], REACH - 1, REACH - 2, total + SUB),
        ):
            main[0, f, near, low - 1 : low + 1, :] = pay[f, at : at + 2, :]
            main[0, f, next_one, low : low + 1, :] = pay[f, at + 2 : at + 3, :]
            main[0, f, near, high : high + 2, :] = pay[f, at + 3 : at + 5, :]
            main[0, f, next_one, high : high + 1, :] = pay[f, at + 5 : at + 6, :]
        for t in range(tiles):
            cut = slice(SUB * t, SUB * (t + 1))
            before, after = pay_refs[0][f, cut, :], pay_refs[1][f, cut, :]
            span = WINDOW * REACH
            left = jnp.where(lane < span, turned(before, -WINDOW * planes), strips_ref[0, f, cut, :])
            strip[0, 0, f, cut, :] = jnp.where(lane >= far, turned(after, far - span), left)
            right = jnp.where(lane < span, before, strips_ref[1, f, cut, :])
            strip[0, 1, f, cut, :] = jnp.where(lane >= far, after, right)
    half = jnp.broadcast_to(0.5 * COURANT / jnp.max(top_ref[...], keepdims=True), (SUB, width))

    def along_y(state, uy, pressure, signal):
        flux = fluxes(state, uy, pressure, 2)
        other = [ahead(v) for v in state]
        flux_other = fluxes(other, ahead(uy), ahead(pressure), 2)
        g = face(flux, flux_other, state, other, signal, ahead(signal))
        return [behind(v) - v for v in g]

    def x_faces(load):
        for t in range(tiles):
            here, there = slice(SUB * t, SUB * (t + 1)), slice(SUB * t + 1, SUB * (t + 1) + 1)
            a, b = load(here), load(there)
            g = face(a[1], b[1], a[0], b[0], a[2], b[2])
            for f in range(5):
                gx[f, SUB * (t + 1) : SUB * (t + 2), :] = g[f]

    def x_change(f, t):
        return (
            gx[f, SUB * (t + 1) - 1 : SUB * (t + 2) - 1, :] - gx[f, SUB * (t + 1) : SUB * (t + 2), :]
        )

    def strip_section(section, side):
        for t in range(tiles):
            cut = slice(SUB * t, SUB * (t + 1))
            state = [strip[section, side, f, cut, :] for f in range(5)]
            ux, uy, uz, pressure, sound = primitives(*state)
            for f, v in enumerate(fluxes(state, ux, pressure, 1)):
                fx[0, f, cut, :] = v
            fx[0, 5, cut, :] = jnp.abs(ux) + sound
            change = along_y(state, uy, pressure, jnp.abs(uy) + sound)
            signal = jnp.abs(uz) + sound
            other = [ahead(v, WINDOW) for v in state]
            g = face(
                fluxes(state, uz, pressure, 3),
                fluxes(other, ahead(uz, WINDOW), ahead(pressure, WINDOW), 3),
                state,
                other,
                signal,
                ahead(signal, WINDOW),
            )
            for f in range(5):
                acc[f, cut, :] = change[f] + (behind(g[f], WINDOW) - g[f])

        def load(cut):
            state = [strip[section, side, f, cut, :] for f in range(5)]
            return state, [fx[0, f, cut, :] for f in range(5)], fx[0, 5, cut, :]

        x_faces(load)
        for t in range(tiles):
            cut = slice(SUB * t, SUB * (t + 1))
            for f in range(5):
                change = half * (acc[f, cut, :] + x_change(f, t))
                here, base = strip[section, side, f, cut, :], strip[0, side, f, cut, :]
                strip[section + 1, side, f, cut, :] = blend(section, base, here, change)

    def plane_values(section, z, slot, t):
        cut = slice(SUB * t, SUB * (t + 1))
        state = [main[section, f, z, cut, :] for f in range(5)]
        ux, uy, uz, pressure, sound = primitives(*state)
        for f, v in enumerate(fluxes(state, ux, pressure, 1)):
            fx[slot, f, cut, :] = v
        fx[slot, 5, cut, :] = jnp.abs(ux) + sound
        fy[slot, 0, cut, :] = uy
        fy[slot, 1, cut, :] = pressure
        fy[slot, 2, cut, :] = jnp.abs(uy) + sound
        flux, signal = fluxes(state, uz, pressure, 3), jnp.abs(uz) + sound
        for f, v in enumerate(flux):
            fz[slot, f, cut, :] = v
        fz[slot, 5, cut, :] = signal
        return state, flux, signal

    def main_section(section, first, last):
        for t in range(tiles):
            plane_values(section, first - 1, (first - 1) % 2, t)

        def plane(z, carry):
            slot = z % 2
            for t in range(tiles):
                cut = slice(SUB * t, SUB * (t + 1))
                state = [main[section, f, z, cut, :] for f in range(5)]
                other, flux_other, signal_other = plane_values(section, z + 1, 1 - slot, t)
                flux = [fz[slot, f, cut, :] for f in range(5)]
                g = face(flux, flux_other, state, other, fz[slot, 5, cut, :], signal_other)
                for f in range(5):
                    acc[f, cut, :] = gz[f, cut, :] - g[f]
                    gz[f, cut, :] = g[f]

            def rest_of_plane():
                def load(cut):
                    state = [main[section, f, z, cut, :] for f in range(5)]
                    return state, [fx[slot, f, cut, :] for f in range(5)], fx[slot, 5, cut, :]

                x_faces(load)
                for t in range(tiles):
                    cut = slice(SUB * t, SUB * (t + 1))
                    state = [main[section, f, z, cut, :] for f in range(5)]
                    sides = along_y(state, *[fy[slot, i, cut, :] for i in range(3)])
                    for f in range(5):
                        change = half * (acc[f, cut, :] + x_change(f, t) + sides[f])
                        base = main[0, f, z, cut, :]
                        main[section + 1, f, z, cut, :] = blend(section, base, state[f], change)

            pl.when(z >= first)(rest_of_plane)
            return carry

        lax.fori_loop(first - 1, last, plane, 0)

    for section in range(3):
        for side in range(2):
            strip_section(section, side)
        main_section(section, 1 + section, planes + 2 * REACH - 1 - section)
    column = lane % WINDOW
    for f in range(5):
        for t in range(rows // SUB):
            cut = slice(SUB * t + REACH, SUB * (t + 1) + REACH)
            edge = jnp.where(
                column < 2 * REACH, strip[3, 1, f, cut, :], behind(strip[3, 0, f, cut, :], REACH)
            )
            for z in range(planes):
                placed = turned(edge, width - REACH - (WINDOW * (z + REACH) + REACH))
                inner = main[3, f, z + REACH, cut, :]
                out_ref[f, z, SUB * t : SUB * (t + 1), :] = jnp.where(
                    (lane < REACH) | (lane >= width - REACH), placed, inner
                )
    for z in range(planes):
        state = [out_ref[f, z] for f in range(5)]
        heat_ref[z] = primitives(*state)[3] / state[0]


def sections(wide, zones, pays, strips, top, rows):
    planes, total, width = wide.shape[1:]
    f32 = jnp.float32
    shared = len(zones) == 1
    tall, deep = total + SUB, planes + 2 * REACH
    args = [wide, *zones, *pays, strips, top]
    return pl.pallas_call(
        functools.partial(section_kernel, shared),
        out_shape=[
            jax.ShapeDtypeStruct((5, planes, rows, width), f32),
            jax.ShapeDtypeStruct((planes, rows, width), f32),
        ],
        in_specs=[VMEM] * len(args),
        out_specs=[VMEM] * 2,
        scratch_shapes=[
            pltpu.VMEM((4, 5, deep, tall, width), f32),
            pltpu.VMEM((4, 2, 5, tall, width), f32),
            pltpu.VMEM((2, 6, tall, width), f32),
            pltpu.VMEM((2, 6, total, width), f32),
            pltpu.VMEM((2, 3, total, width), f32),
            pltpu.VMEM((5, total, width), f32),
            pltpu.VMEM((5, tall, width), f32),
            pltpu.VMEM((5, total, width), f32),
        ],
        name="sections",
    )(*args)


def lanes(values, index):
    return jnp.take_along_axis(values, index, axis=1)

def render_kernel(scale, rho_ref, heat_ref, palette_ref, index_ref, out_ref, table, ke, ko, we, wo):
    planes, rows, width = rho_ref.shape
    count_tf, bins = index_ref.shape
    half = bins // 2
    lane = lax.broadcasted_iota(jnp.int32, (count_tf, half), 1)
    low, high = index_ref[:, :half], index_ref[:, half:]
    for parity in range(2):
        at = lane * 2 + parity
        inside = jnp.where(at < half, at, at - half)
        colour = jnp.where(at < half, lanes(low, inside), lanes(high, inside))
        wrapped = jnp.where(colour < half, colour, colour - half)
        for c in range(4):
            first = jnp.broadcast_to(palette_ref[c:c+1, :half], (count_tf, half))
            second = jnp.broadcast_to(palette_ref[c:c+1, half:], (count_tf, half))
            table[c, parity] = jnp.where(colour < half, lanes(first, wrapped), lanes(second, wrapped))
    def prepare(z, _):
        position = jnp.clip(rho_ref[z] - 0.5, 0.0, 1.0) * (bins - 1)
        cell = jnp.minimum(position.astype(jnp.int32), bins - 2)
        even = (cell + 1) >> 1
        odd = cell >> 1
        ke[z] = even
        ko[z] = odd
        we[z] = 1.0 - jnp.abs(position - (2 * even).astype(jnp.float32))
        wo[z] = 1.0 - jnp.abs(position - (2 * odd + 1).astype(jnp.float32))
        return 0
    lax.fori_loop(0, planes, prepare, 0)
    tables = [[table[c, p] for p in range(2)] for c in range(4)]
    def ray(x, _):
        trans = jnp.ones((count_tf, width), jnp.float32)
        light = [jnp.zeros((count_tf, width), jnp.float32) for _ in range(3)]
        for z in range(planes):
            def wide(ref):
                return jnp.broadcast_to(ref[z, pl.ds(x, 1), :], (count_tf, width))
            ie, io, fe, fo = wide(ke), wide(ko), wide(we), wide(wo)
            looked = [lanes(tables[c][0], ie) * fe + lanes(tables[c][1], io) * fo for c in range(4)]
            passed = jnp.exp(looked[3] * (wide(rho_ref) * -scale))
            weight = trans * (1.0 - passed) * wide(heat_ref)
            light = [light[c] + looked[c] * weight for c in range(3)]
            trans = trans * passed
        for c, values in enumerate(light + [trans]):
            out_ref[pl.ds(c * rows + x, count_tf, stride=4 * rows), :] = values
        return 0
    lax.fori_loop(0, rows, ray, 0)

def render(rho, heat, palette, index, scale):
    planes, rows, width = rho.shape
    count_tf, bins = index.shape
    out = pl.pallas_call(
        lambda *refs: render_kernel(scale, *refs),
        out_shape=jax.ShapeDtypeStruct((count_tf * 4 * rows, width), jnp.float32),
        in_specs=[pl.BlockSpec(memory_space=pltpu.VMEM)] * 4,
        out_specs=pl.BlockSpec(memory_space=pltpu.VMEM),
        scratch_shapes=[pltpu.VMEM((4, 2, count_tf, bins // 2), jnp.float32)]
        + [pltpu.VMEM((planes, rows, width), jnp.int32)] * 2
        + [pltpu.VMEM((planes, rows, width), jnp.float32)] * 2,
        name="render",
    )(rho, heat, palette, index)
    return out.reshape(count_tf, 4, rows, width)


def largest(value, axes):
    for axis in axes:
        size = lax.axis_size(axis)
        step = 1
        while step < size:
            route = [(i, (i + step) % size) for i in range(size)]
            value = jnp.maximum(value, lax.ppermute(value, axis, route))
            step *= 2
    return value


def composed(shares):
    light, passed = None, None
    for d in range(shares.shape[0]):
        slab = shares[d]
        light = slab[:, :3] if d == 0 else light + passed * slab[:, :3]
        passed = slab[:, 3:] if d == 0 else passed * slab[:, 3:]
    return light


def exchanged(shares):
    depth = lax.axis_size("depth")
    count_tf = shares.shape[0]
    per_dev = count_tf // depth
    parts = shares.reshape((depth, per_dev) + shares.shape[1:])
    if depth == 2:
        me = lax.axis_index("depth")
        mine = jnp.where(me == 0, parts[0], parts[1])
        other = lax.ppermute(jnp.where(me == 0, parts[1], parts[0]), "depth", [(0, 1), (1, 0)])
        front = jnp.where(me == 0, mine, other)
        back = jnp.where(me == 0, other, mine)
        return front[:, :3] + front[:, 3:] * back[:, :3]
    return composed(lax.all_to_all(parts, "depth", 0, 0, tiled=True))


def along(axis, distance, wrap):
    size = lax.axis_size(axis)
    if wrap:
        return [(i, (i + distance) % size) for i in range(size)]
    return [(i, i + distance) for i in range(size) if 0 <= i + distance < size]


def shards(density, velocity, pressure, palette, palette_index):
    depth = lax.axis_size("depth")
    planes, rows = density.shape[:2]
    state, zone, low, high, top = opening(density, velocity, pressure)

    def both_ways(block):
        if depth == 2:
            return (lax.ppermute(block, "depth", along("depth", 1, True)),)
        return tuple(lax.ppermute(block, "depth", along("depth", d, True)) for d in (1, -1))

    zones = both_ways(zone)
    from_below = lax.ppermute(high, "group", along("group", 1, False))
    from_above = lax.ppermute(low, "group", along("group", -1, False))
    wide, right, left = windows(state, from_below, from_above)
    from_right = lax.ppermute(right, "image", along("image", -1, True))
    from_left = lax.ppermute(left, "image", along("image", 1, True))
    strips, pay = strips_of(wide, right, left, from_right, from_left)
    pays = both_ways(pay)
    top = largest(top, ("image", "group", "depth"))
    fluid_state, heat = sections(wide, zones, pays, strips, top, rows)
    shares = render(fluid_state[0], heat, palette, palette_index, 2.0 / (planes * depth))
    return (fluid_state, exchanged(shares))


def solution(mesh):
    return jax.shard_map(
        shards,
        mesh=mesh,
        in_specs=(
            P("depth", "group", "image"),
            P(None, "depth", "group", "image"),
            P("depth", "group", "image"),
            P(),
            P(),
        ),
        out_specs=(P(None, "depth", "group", "image"), P("depth", None, "group", "image")),
        check_vma=False,
    )
```

```python
import functools
import math

import jax
import jax.numpy as jnp
from jax import lax
from jax.experimental import pallas as pl
from jax.experimental.pallas import tpu as pltpu
from jax.sharding import PartitionSpec as P

HEAT_RATIO = 1.4
COURANT = 0.8
REACH = 3
WINDOW = 3 * REACH
SUB = 8
VMEM = pl.BlockSpec(memory_space=pltpu.VMEM)
MIB = 1 << 20


def grant(mib):
    return pltpu.CompilerParams(vmem_limit_bytes=mib * MIB)


def ahead(values, distance=1):
    return pltpu.roll(values, values.shape[-1] - distance, axis=values.ndim - 1)


def behind(values, distance=1):
    return pltpu.roll(values, distance, axis=values.ndim - 1)


def turned(values, shift):
    return pltpu.roll(values, shift % values.shape[-1], axis=values.ndim - 1)


def padded_rows(rows):
    return -(-(rows + 2 * REACH) // SUB) * SUB


def primitives(rho, mx, my, mz, energy):
    inverse = 1.0 / rho
    ux, uy, uz = mx * inverse, my * inverse, mz * inverse
    pressure = (HEAT_RATIO - 1.0) * (energy - 0.5 * (mx * ux + my * uy + mz * uz))
    sound = jnp.sqrt(HEAT_RATIO * pressure * inverse)
    return ux, uy, uz, pressure, sound


def fluxes(state, normal, pressure, component):
    rho, mx, my, mz, energy = state
    rows = [state[component], mx * normal, my * normal, mz * normal, (energy + pressure) * normal]
    rows[component] = rows[component] + pressure
    return rows


def face(flux_a, flux_b, state_a, state_b, signal_a, signal_b):
    fastest = jnp.maximum(signal_a, signal_b)
    return [
        (fa + fb) - fastest * (ub - ua)
        for fa, fb, ua, ub in zip(flux_a, flux_b, state_a, state_b)
    ]


def opening_kernel(rho_ref, vel_ref, pre_ref, state_ref, zpay_ref, low_ref, high_ref, top_ref):
    planes, rows, width = rho_ref.shape
    edge = list(range(REACH)) + list(range(planes - REACH, planes))
    fastest = None
    for z in range(planes):
        rho, p = rho_ref[z], pre_ref[z]
        v = [vel_ref[i, z] for i in range(3)]
        signal = jnp.abs(v[0]) + jnp.abs(v[1]) + jnp.abs(v[2]) + 3.0 * jnp.sqrt(HEAT_RATIO * p / rho)
        signal = jnp.max(signal.reshape(rows // SUB, SUB, width), axis=0)
        fastest = signal if fastest is None else jnp.maximum(fastest, signal)
        kinetic = 0.5 * rho * (v[0] * v[0] + v[1] * v[1] + v[2] * v[2])
        fields = [rho, rho * v[0], rho * v[1], rho * v[2], p / (HEAT_RATIO - 1.0) + kinetic]
        for f in range(5):
            state_ref[f, z] = fields[f]
            if z in edge:
                zpay_ref[f, edge.index(z)] = fields[f]
            at = (f * planes + z) * REACH
            low_ref[at : at + REACH, :] = fields[f][:REACH]
            high_ref[at : at + REACH, :] = fields[f][rows - REACH :]
    top_ref[...] = fastest
    for ref in (low_ref, high_ref):
        ref[5 * planes * REACH :, :] = fastest


def opening(density, velocity, pressure):
    planes, rows, width = density.shape
    f32 = jnp.float32
    return pl.pallas_call(
        opening_kernel,
        out_shape=[
            jax.ShapeDtypeStruct((5, planes, rows, width), f32),
            jax.ShapeDtypeStruct((5, 2 * REACH, rows, width), f32),
            jax.ShapeDtypeStruct((5 * planes * REACH + SUB, width), f32),
            jax.ShapeDtypeStruct((5 * planes * REACH + SUB, width), f32),
            jax.ShapeDtypeStruct((SUB, width), f32),
        ],
        in_specs=[VMEM] * 3,
        out_specs=[VMEM] * 5,
        name="opening",
        compiler_params=grant(8),
    )(density, velocity, pressure)


def window_kernel(
    state_ref, low_ref, high_ref, top_ref, wide_ref, right_ref, left_ref, peak_ref
):
    planes, rows, width = state_ref.shape[1:]
    sent = slice(5 * planes * REACH, 5 * planes * REACH + SUB)
    peak_ref[...] = jnp.maximum(top_ref[...], jnp.maximum(low_ref[sent, :], high_ref[sent, :]))
    total = wide_ref.shape[2]
    group, groups = lax.axis_index("group"), lax.axis_size("group")
    lane = lax.broadcasted_iota(jnp.int32, (SUB, width), 1)
    for f in range(5):
        sign = -1.0 if f == 1 else 1.0
        for z in range(planes):
            at = (f * planes + z) * REACH
            wide_ref[f, z, REACH : REACH + rows, :] = state_ref[f, z]
            mirrored = [state_ref[f, z, r : r + 1, :] * sign for r in range(REACH - 1, -1, -1)]
            below = jnp.where(group == 0, jnp.concatenate(mirrored, axis=0), low_ref[at : at + REACH, :])
            wide_ref[f, z, :REACH, :] = below
            mirrored = [state_ref[f, z, rows - 1 - r : rows - r, :] * sign for r in range(REACH)]
            above = jnp.where(
                group == groups - 1, jnp.concatenate(mirrored, axis=0), high_ref[at : at + REACH, :]
            )
            wide_ref[f, z, REACH + rows : 2 * REACH + rows, :] = above

    def fields(f, carry):
        for t in range(total // SUB):
            cut = slice(SUB * t, SUB * (t + 1))
            right = jnp.zeros((SUB, width), jnp.float32)
            left = right
            for z in range(planes):
                start = WINDOW * (z + REACH)
                inside = (lane >= start) & (lane < start + WINDOW)
                values = wide_ref[f, z, cut, :]
                right = jnp.where(inside, turned(values, start - (width - 2 * REACH)), right)
                left = jnp.where(inside, turned(values, start - (width - REACH)), left)
            right_ref[f, cut, :] = right
            left_ref[f, cut, :] = left
        return carry

    lax.fori_loop(0, 5, fields, 0)


def windows(state, low, high, top):
    planes, rows, width = state.shape[1:]
    total = padded_rows(rows)
    f32 = jnp.float32
    return pl.pallas_call(
        window_kernel,
        out_shape=[
            jax.ShapeDtypeStruct((5, planes, total, width), f32),
            jax.ShapeDtypeStruct((5, total, width), f32),
            jax.ShapeDtypeStruct((5, total, width), f32),
            jax.ShapeDtypeStruct((SUB, width), f32),
        ],
        in_specs=[VMEM] * 4,
        out_specs=[VMEM] * 4,
        name="windows",
        compiler_params=grant(8),
    )(state, low, high, top)


def strip_kernel(wide_ref, right_ref, left_ref, from_right, from_left, strips_ref, pay_ref):
    planes, total, width = wide_ref.shape[1:]
    rows = total - 2 * REACH - (total - 2 * REACH) % SUB
    lane = lax.broadcasted_iota(jnp.int32, (SUB, width), 1)
    column = lane % WINDOW
    span = WINDOW * REACH
    first, last = WINDOW * REACH, WINDOW * planes
    far = WINDOW * (REACH + planes)
    for f in range(5):
        for t in range(total // SUB):
            cut = slice(SUB * t, SUB * (t + 1))
            right = jnp.where(column >= 2 * REACH, from_right[f, cut, :], right_ref[f, cut, :])
            left = jnp.where(column < REACH, from_left[f, cut, :], left_ref[f, cut, :])
            strips_ref[0, f, cut, :] = left
            strips_ref[1, f, cut, :] = right
            sent = jnp.where(lane < span, turned(right, -last), left)
            pay_ref[f, cut, :] = jnp.where(lane >= far, turned(right, far - first), sent)
        low, high = REACH - 1, REACH + rows
        for side, (near, next_one) in enumerate(((0, 1), (planes - 1, planes - 2))):
            at = total + SUB * side
            pay_ref[f, at : at + 2, :] = wide_ref[f, near, low - 1 : low + 1, :]
            pay_ref[f, at + 2 : at + 3, :] = wide_ref[f, next_one, low : low + 1, :]
            pay_ref[f, at + 3 : at + 5, :] = wide_ref[f, near, high : high + 2, :]
            pay_ref[f, at + 5 : at + 6, :] = wide_ref[f, next_one, high : high + 1, :]
            pay_ref[f, at + 6 : at + 8, :] = jnp.zeros((2, width), jnp.float32)


def strips_of(wide, right, left, from_right, from_left):
    planes, total, width = wide.shape[1:]
    f32 = jnp.float32
    return pl.pallas_call(
        strip_kernel,
        out_shape=[
            jax.ShapeDtypeStruct((2, 5, total, width), f32),
            jax.ShapeDtypeStruct((5, total + 2 * SUB, width), f32),
        ],
        in_specs=[VMEM] * 5,
        out_specs=[VMEM] * 2,
        name="strips",
        compiler_params=grant(8),
    )(wide, right, left, from_right, from_left)


def blend(section, base, here, change, half):
    if section == 0:
        return here + half * change
    if section == 1:
        return 0.75 * base + 0.25 * (here + half * change)
    return base * (1.0 / 3.0) + (2.0 / 3.0) * (here + half * change)


def along_y(state, flux, uy, pressure, signal):
    other = [ahead(v) for v in state]
    flux_other = fluxes(other, ahead(uy), ahead(pressure), 2)
    g = face(flux, flux_other, state, other, signal, ahead(signal))
    return [behind(v) - v for v in g]


def section_kernel(shared, *refs):
    if shared:
        wide_ref, zone_ref, pay_ref, strips_ref, top_ref = refs[:5]
        zone_refs, pay_refs = (zone_ref, zone_ref), (pay_ref, pay_ref)
        rest = refs[5:]
    else:
        wide_ref, strips_ref, top_ref = refs[0], refs[5], refs[6]
        zone_refs, pay_refs = refs[1:3], refs[3:5]
        rest = refs[7:]
    out_ref, rho_ref, heat_ref = rest[:3]
    main, strip, (fx, gx, acc, fz, gz) = rest[3:7], rest[7:11], rest[11:]
    planes, total, width = wide_ref.shape[1:]
    rows = out_ref.shape[2]
    tiles = total // SUB
    lane = lax.broadcasted_iota(jnp.int32, (SUB, width), 1)
    far = WINDOW * (REACH + planes)
    for f in range(5):
        for z in range(planes):
            main[0][f, z + REACH, :total, :] = wide_ref[f, z]
        for z in range(REACH):
            main[0][f, z, REACH : REACH + rows, :] = zone_refs[0][f, REACH + z]
            main[0][f, planes + REACH + z, REACH : REACH + rows, :] = zone_refs[1][f, z]
        low, high = REACH - 1, REACH + rows
        for pay, near, next_one, at in (
            (pay_refs[1], planes + REACH, planes + REACH + 1, total),
            (pay_refs[0], REACH - 1, REACH - 2, total + SUB),
        ):
            main[0][f, near, low - 1 : low + 1, :] = pay[f, at : at + 2, :]
            main[0][f, next_one, low : low + 1, :] = pay[f, at + 2 : at + 3, :]
            main[0][f, near, high : high + 2, :] = pay[f, at + 3 : at + 5, :]
            main[0][f, next_one, high : high + 1, :] = pay[f, at + 5 : at + 6, :]
        for t in range(tiles):
            cut = slice(SUB * t, SUB * (t + 1))
            before, after = pay_refs[0][f, cut, :], pay_refs[1][f, cut, :]
            span = WINDOW * REACH
            left = jnp.where(lane < span, turned(before, -WINDOW * planes), strips_ref[0, f, cut, :])
            strip[0][0, f, cut, :] = jnp.where(lane >= far, turned(after, far - span), left)
            right = jnp.where(lane < span, before, strips_ref[1, f, cut, :])
            strip[0][1, f, cut, :] = jnp.where(lane >= far, after, right)
    half = jnp.broadcast_to(0.5 * COURANT / jnp.max(top_ref[...], keepdims=True), (SUB, width))

    def x_pass(which, load, t):
        here, there = slice(SUB * t, SUB * (t + 1)), slice(SUB * t + 1, SUB * (t + 1) + 1)
        a, b = load(here), load(there)
        g = face(
            [fx[which, f, here, :] for f in range(5)],
            [fx[which, f, there, :] for f in range(5)],
            a,
            b,
            fx[which, 5, here, :],
            fx[which, 5, there, :],
        )
        for f in range(5):
            gx[which, f, SUB * (t + 1) : SUB * (t + 2), :] = g[f]
            below = gx[which, f, SUB * (t + 1) - 1 : SUB * (t + 2) - 1, :]
            acc[which, f, here, :] = acc[which, f, here, :] + (below - g[f])

    def keep_x(which, state, ux, pressure, sound, cut):
        for f, v in enumerate(fluxes(state, ux, pressure, 1)):
            fx[which, f, cut, :] = v
        fx[which, 5, cut, :] = jnp.abs(ux) + sound

    def strip_section(section, side):
        source, target = strip[section], strip[section + 1]

        def load(cut):
            return [source[side, f, cut, :] for f in range(5)]

        def finish(t):
            cut = slice(SUB * t, SUB * (t + 1))
            x_pass(side, load, t)
            for f in range(5):
                here, base = source[side, f, cut, :], strip[0][side, f, cut, :]
                target[side, f, cut, :] = blend(section, base, here, acc[side, f, cut, :], half)

        for t in range(tiles):
            cut = slice(SUB * t, SUB * (t + 1))
            state = load(cut)
            ux, uy, uz, pressure, sound = primitives(*state)
            keep_x(side, state, ux, pressure, sound, cut)
            change = along_y(state, fluxes(state, uy, pressure, 2), uy, pressure, jnp.abs(uy) + sound)
            signal = jnp.abs(uz) + sound
            other = [ahead(v, WINDOW) for v in state]
            g = face(
                fluxes(state, uz, pressure, 3),
                fluxes(other, ahead(uz, WINDOW), ahead(pressure, WINDOW), 3),
                state,
                other,
                signal,
                ahead(signal, WINDOW),
            )
            for f in range(5):
                acc[side, f, cut, :] = change[f] + (behind(g[f], WINDOW) - g[f])
            if t:
                finish(t - 1)
        finish(tiles - 1)

    def main_section(section, first, last):
        source, target, base = main[section], main[section + 1], main[0]

        def plane(w, with_face, with_finish, with_sides):
            def load(cut):
                return [source[f, w, cut, :] for f in range(5)]

            for t in range(tiles):
                cut = slice(SUB * t, SUB * (t + 1))
                state = load(cut)
                ux, uy, uz, pressure, sound = primitives(*state)
                flux, signal = fluxes(state, uz, pressure, 3), jnp.abs(uz) + sound
                if with_face:
                    before = [source[f, w - 1, cut, :] for f in range(5)]
                    flux_before = [fz[f, cut, :] for f in range(5)]
                    g = face(flux_before, flux, before, state, fz[5, cut, :], signal)
                    for f in range(5):
                        if with_finish:
                            change = acc[0, f, cut, :] + (gz[f, cut, :] - g[f])
                            started = base[f, w - 1, cut, :] if section else None
                            target[f, w - 1, cut, :] = blend(section, started, before[f], change, half)
                        if with_sides:
                            gz[f, cut, :] = g[f]
                if with_sides or not with_face:
                    for f in range(5):
                        fz[f, cut, :] = flux[f]
                    fz[5, cut, :] = signal
                if with_sides:
                    keep_x(0, state, ux, pressure, sound, cut)
                    flux = fluxes(state, uy, pressure, 2)
                    change = along_y(state, flux, uy, pressure, jnp.abs(uy) + sound)
                    for f in range(5):
                        acc[0, f, cut, :] = change[f]
                    if t:
                        x_pass(0, load, t - 1)
            if with_sides:
                x_pass(0, load, tiles - 1)

        plane(first - 1, False, False, False)
        plane(first, True, False, True)

        def step(w, carry):
            plane(w, True, True, True)
            return carry

        lax.fori_loop(first + 1, last, step, 0)
        plane(last, True, True, False)

    for section in range(3):
        for side in range(2):
            strip_section(section, side)
        main_section(section, 1 + section, planes + 2 * REACH - 1 - section)
    column = lane % WINDOW
    for f in range(5):
        for t in range(rows // SUB):
            cut = slice(SUB * t + REACH, SUB * (t + 1) + REACH)
            edge = jnp.where(
                column < 2 * REACH, strip[3][1, f, cut, :], behind(strip[3][0, f, cut, :], REACH)
            )
            for z in range(planes):
                placed = turned(edge, width - REACH - (WINDOW * (z + REACH) + REACH))
                inner = main[3][f, z + REACH, cut, :]
                out_ref[f, z, SUB * t : SUB * (t + 1), :] = jnp.where(
                    (lane < REACH) | (lane >= width - REACH), placed, inner
                )
    for z in range(planes):
        state = [out_ref[f, z] for f in range(5)]
        rho_ref[z] = state[0]
        heat_ref[z] = primitives(*state)[3] / state[0]


def sections(wide, zones, pays, strips, top, rows):
    planes, total, width = wide.shape[1:]
    f32 = jnp.float32
    shared = len(zones) == 1
    tall, deep = total + SUB, planes + 2 * REACH
    args = [wide, *zones, *pays, strips, top]
    brick = jax.ShapeDtypeStruct((planes, rows, width), f32)
    return pl.pallas_call(
        functools.partial(section_kernel, shared),
        out_shape=[jax.ShapeDtypeStruct((5, planes, rows, width), f32), brick, brick],
        in_specs=[VMEM] * len(args),
        out_specs=[VMEM] * 3,
        scratch_shapes=[pltpu.VMEM((5, deep, tall, width), f32)] * 4
        + [pltpu.VMEM((2, 5, tall, width), f32)] * 4
        + [
            pltpu.VMEM((2, 6, tall, width), f32),
            pltpu.VMEM((2, 5, tall, width), f32),
            pltpu.VMEM((2, 5, total, width), f32),
            pltpu.VMEM((6, total, width), f32),
            pltpu.VMEM((5, total, width), f32),
        ],
        name="sections",
        compiler_params=grant(24),
    )(*args)


def lanes(values, index):
    return lax.gather(
        values,
        index[..., None],
        lax.GatherDimensionNumbers(
            offset_dims=(),
            collapsed_slice_dims=(1,),
            start_index_map=(1,),
            operand_batching_dims=(0,),
            start_indices_batching_dims=(0,),
        ),
        slice_sizes=(1, 1),
        mode=lax.GatherScatterMode.PROMISE_IN_BOUNDS,
    )


LEVELS = 65535


def render_kernel(
    scale, begin, count, halves, rho_ref, heat_ref, palette_ref, index_ref, *refs
):
    outs, (table, ke, ko, we, wo, thick) = refs[: len(refs) - 6], refs[len(refs) - 6 :]
    planes, rows, width = rho_ref.shape
    count_tf, bins = index_ref.shape
    half = bins // 2
    chosen = index_ref[...]
    if halves:
        swapped = pltpu.roll(chosen, count_tf // 2, axis=0)
        chosen = jnp.where(lax.axis_index("depth") == 0, swapped, chosen)
    colours = palette_ref[...]
    least = jnp.min(colours, keepdims=True)
    step = jnp.maximum(jnp.max(colours, keepdims=True) - least, 1e-6) * (1.0 / LEVELS)
    coded = ((colours - least) / step + 0.5).astype(jnp.int32)
    words = [(coded[c : c + 1] - (LEVELS + 1) // 2) * (LEVELS + 1) + coded[c + 1 : c + 2] for c in (0, 2)]
    lane = lax.broadcasted_iota(jnp.int32, (count_tf, half), 1)
    low, high = chosen[:, :half], chosen[:, half:]
    for parity in range(2):
        at = lane * 2 + parity
        inside = jnp.where(at < half, at, at - half)
        colour = jnp.where(at < half, lanes(low, inside), lanes(high, inside))
        wrapped = jnp.where(colour < half, colour, colour - half)
        for pair in range(2):
            first = jnp.broadcast_to(words[pair][:, :half], (count_tf, half))
            second = jnp.broadcast_to(words[pair][:, half:], (count_tf, half))
            table[pair, parity] = jnp.where(
                colour < half, lanes(first, wrapped), lanes(second, wrapped)
            )
    step_wide = jnp.broadcast_to(step, (SUB, width))
    for z in range(planes):
        for t in range(count // SUB):
            cut, from_cut = slice(SUB * t, SUB * (t + 1)), slice(begin + SUB * t, begin + SUB * (t + 1))
            rho = rho_ref[z, from_cut, :]
            position = jnp.clip(rho - 0.5, 0.0, 1.0) * (bins - 1)
            cell = jnp.minimum(position.astype(jnp.int32), bins - 2)
            even = (cell + 1) >> 1
            odd = cell >> 1
            ke[z, cut, :] = even
            ko[z, cut, :] = odd
            we[z, cut, :] = (1.0 - jnp.abs(position - (2 * even).astype(jnp.float32))) * step_wide
            wo[z, cut, :] = (1.0 - jnp.abs(position - (2 * odd + 1).astype(jnp.float32))) * step_wide
            thick[z, cut, :] = rho * (-scale * math.log2(math.e))
    tables = [[table[pair, p] for p in range(2)] for pair in range(2)]
    base_low = jnp.broadcast_to(least, (count_tf, width))
    base_high = base_low + jnp.broadcast_to(step, (count_tf, width)) * ((LEVELS + 1) // 2)

    def ray(x, carry):
        trans = jnp.ones((count_tf, width), jnp.float32)
        light = [jnp.zeros((count_tf, width), jnp.float32) for _ in range(3)]
        for z in range(planes):

            def wide(ref, at=x):
                return jnp.broadcast_to(ref[z, pl.ds(at, 1), :], (count_tf, width))

            ie, io, fe, fo = wide(ke), wide(ko), wide(we), wide(wo)
            looked = []
            for pair in range(2):
                even, odd = lanes(tables[pair][0], ie), lanes(tables[pair][1], io)
                looked.append(
                    base_high
                    + (even >> 16).astype(jnp.float32) * fe
                    + (odd >> 16).astype(jnp.float32) * fo
                )
                looked.append(
                    base_low
                    + (even & LEVELS).astype(jnp.float32) * fe
                    + (odd & LEVELS).astype(jnp.float32) * fo
                )
            passed = trans * jnp.exp2(looked[3] * wide(thick))
            weight = (trans - passed) * wide(heat_ref, x + begin)
            light = [light[c] + looked[c] * weight for c in range(3)]
            trans = passed
        per_out = count_tf // len(outs)
        for c, values in enumerate(light + [trans]):
            for i, out in enumerate(outs):
                out[pl.ds(c * count + x, per_out, stride=4 * count), :] = values[
                    per_out * i : per_out * (i + 1)
                ]
        return carry

    lax.fori_loop(0, count, ray, 0)


def render(rho, heat, palette, index, scale, begin, count, halves):
    planes, rows, width = rho.shape
    count_tf, bins = index.shape
    parts = 2 if halves else 1
    per_out = count_tf // parts
    shape = jax.ShapeDtypeStruct((per_out * 4 * count, width), jnp.float32)
    scratch = [pltpu.VMEM((planes, count, width), t) for t in (jnp.int32,) * 2 + (jnp.float32,) * 3]
    outs = pl.pallas_call(
        functools.partial(render_kernel, scale, begin, count, halves),
        out_shape=[shape] * parts,
        in_specs=[VMEM] * 4,
        out_specs=[VMEM] * parts,
        scratch_shapes=[pltpu.VMEM((2, 2, count_tf, bins // 2), jnp.int32)] + scratch,
        name=f"render_{begin}",
        compiler_params=grant(8),
    )(rho, heat, palette, index)
    return [out.reshape(per_out, 4, count, width) for out in outs]


def exchange_max(value, axis, step):
    size = lax.axis_size(axis)
    if size & (size - 1) == 0:
        route = [(i, i ^ step) for i in range(size)]
    else:
        route = along(axis, step, True)
    return jnp.maximum(value, lax.ppermute(value, axis, route))


def largest(value, axis, step=1):
    while step < lax.axis_size(axis):
        value = exchange_max(value, axis, step)
        step *= 2
    return value


def composed(shares):
    light, passed = None, None
    for d in range(shares.shape[0]):
        slab = shares[d]
        light = slab[:, :3] if d == 0 else light + passed * slab[:, :3]
        passed = slab[:, 3:] if d == 0 else passed * slab[:, 3:]
    return light


def along(axis, distance, wrap):
    size = lax.axis_size(axis)
    if wrap:
        return [(i, (i + distance) % size) for i in range(size)]
    return [(i, i + distance) for i in range(size) if 0 <= i + distance < size]


def pictured(rho, heat, palette, index):
    depth = lax.axis_size("depth")
    planes, rows, _ = rho.shape
    scale = 2.0 / (planes * depth)
    if depth != 2:
        (shares,) = render(rho, heat, palette, index, scale, 0, rows, False)
        parts = shares.reshape((depth, shares.shape[0] // depth) + shares.shape[1:])
        return composed(lax.all_to_all(parts, "depth", 0, 0, tiled=True))
    chunk = rows // 2 if rows % (2 * SUB) == 0 else rows
    kept, sent = [], []
    for begin in range(0, rows, chunk):
        other, own = render(rho, heat, palette, index, scale, begin, chunk, True)
        kept.append(own)
        sent.append(lax.ppermute(other, "depth", along("depth", 1, True)))
    in_front = lax.axis_index("depth") == 0
    pieces = []
    for own, other in zip(kept, sent):
        front, back = jnp.where(in_front, own, other), jnp.where(in_front, other, own)
        pieces.append(front[:, :3] + front[:, 3:] * back[:, :3])
    return jnp.concatenate(pieces, axis=2)


def shards(density, velocity, pressure, palette, palette_index):
    depth, groups = lax.axis_size("depth"), lax.axis_size("group")
    planes, rows = density.shape[:2]
    state, zone, low, high, top = opening(density, velocity, pressure)

    def both_ways(block):
        if depth == 2:
            return (lax.ppermute(block, "depth", along("depth", 1, True)),)
        return tuple(lax.ppermute(block, "depth", along("depth", d, True)) for d in (1, -1))

    zones = both_ways(zone)
    from_below = lax.ppermute(high, "group", along("group", 1, False))
    from_above = lax.ppermute(low, "group", along("group", -1, False))
    wide, right, left, top = windows(state, from_below, from_above, top)
    from_right = lax.ppermute(right, "image", along("image", -1, True))
    from_left = lax.ppermute(left, "image", along("image", 1, True))
    if groups == 4:
        top = exchange_max(top, "group", 2)
    else:
        top = largest(top, "group")
    top = exchange_max(top, "image", 1)
    from_right, from_left, top = lax.optimization_barrier((from_right, from_left, top))
    strips, pay = strips_of(wide, right, left, from_right, from_left)
    pays = both_ways(pay)
    top = largest(largest(top, "image", 2), "depth")
    fluid_state, rho, heat = sections(wide, zones, pays, strips, top, rows)
    return (fluid_state, pictured(rho, heat, palette, palette_index))


def solution(mesh):
    return jax.shard_map(
        shards,
        mesh=mesh,
        in_specs=(
            P("depth", "group", "image"),
            P(None, "depth", "group", "image"),
            P("depth", "group", "image"),
            P(),
            P(),
        ),
        out_specs=(P(None, "depth", "group", "image"), P("depth", None, "group", "image")),
        check_vma=False,
    )
```

```python
import functools
import math

import jax
import jax.numpy as jnp
from jax import lax
from jax.experimental import pallas as pl
from jax.experimental.pallas import tpu as pltpu
from jax.sharding import PartitionSpec as P


HEAT_RATIO = 1.4
COURANT = 0.8
REACH = 3
WINDOW = 3 * REACH
SUB = 8
PIECES = 3
VMEM = pl.BlockSpec(memory_space=pltpu.VMEM)
MIB = 1 << 20


def grant(mib):
    return pltpu.CompilerParams(vmem_limit_bytes=mib * MIB)


def ahead(values, distance=1):
    return pltpu.roll(values, values.shape[-1] - distance, axis=values.ndim - 1)


def behind(values, distance=1):
    return pltpu.roll(values, distance, axis=values.ndim - 1)


def turned(values, shift):
    return pltpu.roll(values, shift % values.shape[-1], axis=values.ndim - 1)


def padded_rows(rows):
    return -(-(rows + 2 * REACH) // SUB) * SUB


def primitives(rho, mx, my, mz, energy):
    inverse = 1.0 / rho
    ux, uy, uz = mx * inverse, my * inverse, mz * inverse
    pressure = (HEAT_RATIO - 1.0) * (energy - 0.5 * (mx * ux + my * uy + mz * uz))
    sound = jnp.sqrt(HEAT_RATIO * pressure * inverse)
    return ux, uy, uz, pressure, sound


def fluxes(state, normal, pressure, component):
    _, mx, my, mz, energy = state
    rows = [state[component], mx * normal, my * normal, mz * normal, (energy + pressure) * normal]
    rows[component] = rows[component] + pressure
    return rows


def face(flux_a, flux_b, state_a, state_b, signal_a, signal_b):
    fastest = jnp.maximum(signal_a, signal_b)
    return [
        (fa + fb) - fastest * (ub - ua)
        for fa, fb, ua, ub in zip(flux_a, flux_b, state_a, state_b)
    ]


def opening_kernel(
    rho_hbm, vel_hbm, pre_hbm, state_ref, zpay_ref, low_ref, high_ref, top_ref, rho_ref, vel_ref, pre_ref, sems
):
    planes, rows, width = rho_ref.shape
    pairs = ((rho_hbm, rho_ref), (vel_hbm, vel_ref), (pre_hbm, pre_ref))
    copies = [pltpu.make_async_copy(src, dst, sems.at[i]) for i, (src, dst) in enumerate(pairs)]
    for copy in copies:
        copy.start()
    for copy in copies:
        copy.wait()
    edge = list(range(REACH)) + list(range(planes - REACH, planes))
    fastest = None
    for z in range(planes):
        rho, p = rho_ref[z], pre_ref[z]
        v = [vel_ref[i, z] for i in range(3)]
        signal = jnp.abs(v[0]) + jnp.abs(v[1]) + jnp.abs(v[2]) + 3.0 * jnp.sqrt(HEAT_RATIO * p / rho)
        signal = jnp.max(signal.reshape(rows // SUB, SUB, width), axis=0)
        fastest = signal if fastest is None else jnp.maximum(fastest, signal)
        kinetic = 0.5 * rho * (v[0] * v[0] + v[1] * v[1] + v[2] * v[2])
        fields = [rho, rho * v[0], rho * v[1], rho * v[2], p / (HEAT_RATIO - 1.0) + kinetic]
        for f in range(5):
            state_ref[f, z] = fields[f]
            if z in edge:
                zpay_ref[f, edge.index(z)] = fields[f]
            at = (f * planes + z) * REACH
            low_ref[at : at + REACH, :] = fields[f][:REACH]
            high_ref[at : at + REACH, :] = fields[f][rows - REACH :]
    top_ref[...] = fastest
    for ref in (low_ref, high_ref):
        ref[5 * planes * REACH :, :] = fastest


def opening(density, velocity, pressure):
    planes, rows, width = density.shape
    f32 = jnp.float32
    return pl.pallas_call(
        opening_kernel,
        out_shape=[
            jax.ShapeDtypeStruct((5, planes, rows, width), f32),
            jax.ShapeDtypeStruct((5, 2 * REACH, rows, width), f32),
            jax.ShapeDtypeStruct((5 * planes * REACH + SUB, width), f32),
            jax.ShapeDtypeStruct((5 * planes * REACH + SUB, width), f32),
            jax.ShapeDtypeStruct((SUB, width), f32),
        ],
        in_specs=[pl.BlockSpec(memory_space=pltpu.HBM)] * 3,
        out_specs=[VMEM] * 5,
        scratch_shapes=[
            pltpu.VMEM(density.shape, f32),
            pltpu.VMEM(velocity.shape, f32),
            pltpu.VMEM(pressure.shape, f32),
            pltpu.SemaphoreType.DMA((3,)),
        ],
        name="opening",
        compiler_params=grant(8),
    )(*[pltpu.with_memory_space_constraint(a, pltpu.HBM) for a in (density, velocity, pressure)])


def window_kernel(
    state_ref, low_ref, high_ref, top_ref, wide_ref, right_ref, left_ref, peak_ref
):
    planes, rows, width = state_ref.shape[1:]
    sent = slice(5 * planes * REACH, 5 * planes * REACH + SUB)
    peak_ref[...] = jnp.maximum(top_ref[...], jnp.maximum(low_ref[sent, :], high_ref[sent, :]))
    total = wide_ref.shape[2]
    group, groups = lax.axis_index("group"), lax.axis_size("group")
    lane = lax.broadcasted_iota(jnp.int32, (SUB, width), 1)
    for f in range(5):
        sign = -1.0 if f == 1 else 1.0
        for z in range(planes):
            at = (f * planes + z) * REACH
            wide_ref[f, z, REACH : REACH + rows, :] = state_ref[f, z]
            mirrored = [state_ref[f, z, r : r + 1, :] * sign for r in range(REACH - 1, -1, -1)]
            below = jnp.where(group == 0, jnp.concatenate(mirrored, axis=0), low_ref[at : at + REACH, :])
            wide_ref[f, z, :REACH, :] = below
            mirrored = [state_ref[f, z, rows - 1 - r : rows - r, :] * sign for r in range(REACH)]
            above = jnp.where(
                group == groups - 1, jnp.concatenate(mirrored, axis=0), high_ref[at : at + REACH, :]
            )
            wide_ref[f, z, REACH + rows : 2 * REACH + rows, :] = above

    def fields(f, carry):
        for t in range(total // SUB):
            cut = slice(SUB * t, SUB * (t + 1))
            right = jnp.zeros((SUB, width), jnp.float32)
            left = right
            for z in range(planes):
                start = WINDOW * (z + REACH)
                inside = (lane >= start) & (lane < start + WINDOW)
                values = wide_ref[f, z, cut, :]
                right = jnp.where(inside, turned(values, start - (width - 2 * REACH)), right)
                left = jnp.where(inside, turned(values, start - (width - REACH)), left)
            right_ref[f, cut, :] = right
            left_ref[f, cut, :] = left
        return carry

    lax.fori_loop(0, 5, fields, 0)


def windows(state, low, high, top):
    planes, rows, width = state.shape[1:]
    total = padded_rows(rows)
    f32 = jnp.float32
    return pl.pallas_call(
        window_kernel,
        out_shape=[
            jax.ShapeDtypeStruct((5, planes, total, width), f32),
            jax.ShapeDtypeStruct((5, total, width), f32),
            jax.ShapeDtypeStruct((5, total, width), f32),
            jax.ShapeDtypeStruct((SUB, width), f32),
        ],
        in_specs=[VMEM] * 4,
        out_specs=[VMEM] * 4,
        name="windows",
        compiler_params=grant(8),
    )(state, low, high, top)


def strip_kernel(wide_ref, right_ref, left_ref, from_right, from_left, strips_ref, pay_ref):
    planes, total, width = wide_ref.shape[1:]
    rows = total - 2 * REACH - (total - 2 * REACH) % SUB
    lane = lax.broadcasted_iota(jnp.int32, (SUB, width), 1)
    column = lane % WINDOW
    span = WINDOW * REACH
    first, last = WINDOW * REACH, WINDOW * planes
    far = WINDOW * (REACH + planes)
    for f in range(5):
        for t in range(total // SUB):
            cut = slice(SUB * t, SUB * (t + 1))
            right = jnp.where(column >= 2 * REACH, from_right[f, cut, :], right_ref[f, cut, :])
            left = jnp.where(column < REACH, from_left[f, cut, :], left_ref[f, cut, :])
            strips_ref[0, f, cut, :] = left
            strips_ref[1, f, cut, :] = right
            sent = jnp.where(lane < span, turned(right, -last), left)
            pay_ref[f, cut, :] = jnp.where(lane >= far, turned(right, far - first), sent)
        low, high = REACH - 1, REACH + rows
        for side, (near, next_one) in enumerate(((0, 1), (planes - 1, planes - 2))):
            at = total + SUB * side
            pay_ref[f, at : at + 2, :] = wide_ref[f, near, low - 1 : low + 1, :]
            pay_ref[f, at + 2 : at + 3, :] = wide_ref[f, next_one, low : low + 1, :]
            pay_ref[f, at + 3 : at + 5, :] = wide_ref[f, near, high : high + 2, :]
            pay_ref[f, at + 5 : at + 6, :] = wide_ref[f, next_one, high : high + 1, :]
            pay_ref[f, at + 6 : at + 8, :] = jnp.zeros((2, width), jnp.float32)


def strips_of(wide, right, left, from_right, from_left):
    _, total, width = wide.shape[1:]
    f32 = jnp.float32
    return pl.pallas_call(
        strip_kernel,
        out_shape=[
            jax.ShapeDtypeStruct((2, 5, total, width), f32),
            jax.ShapeDtypeStruct((5, total + 2 * SUB, width), f32),
        ],
        in_specs=[VMEM] * 5,
        out_specs=[VMEM] * 2,
        name="strips",
        compiler_params=grant(8),
    )(wide, right, left, from_right, from_left)


def blend(section, base, here, change, half):
    if section == 0:
        return here + half * change
    if section == 1:
        return 0.75 * base + 0.25 * (here + half * change)
    return base * (1.0 / 3.0) + (2.0 / 3.0) * (here + half * change)


def along_y(state, flux, uy, pressure, signal):
    other = [ahead(v) for v in state]
    flux_other = fluxes(other, ahead(uy), ahead(pressure), 2)
    g = face(flux, flux_other, state, other, signal, ahead(signal))
    return [behind(v) - v for v in g]


def section_kernel(shared, *refs):
    if shared:
        wide_ref, zone_ref, pay_ref, strips_ref, top_ref = refs[:5]
        zone_refs, pay_refs = (zone_ref, zone_ref), (pay_ref, pay_ref)
        rest = refs[5:]
    else:
        wide_ref, strips_ref, top_ref = refs[0], refs[5], refs[6]
        zone_refs, pay_refs = refs[1:3], refs[3:5]
        rest = refs[7:]
    out_ref, rho_ref, heat_ref = rest[:3]
    main, strip, (fx, gx, acc, fz, gz) = rest[3:7], rest[7:11], rest[11:16]
    strip_buffers = (rest[16:19], rest[19:22])
    planes, total, width = wide_ref.shape[1:]
    rows = out_ref.shape[2]
    tiles = total // SUB
    lane = lax.broadcasted_iota(jnp.int32, (SUB, width), 1)
    far = WINDOW * (REACH + planes)
    for f in range(5):
        for z in range(planes):
            main[0][f, z + REACH, :total, :] = wide_ref[f, z]
        for z in range(REACH):
            main[0][f, z, REACH : REACH + rows, :] = zone_refs[0][f, REACH + z]
            main[0][f, planes + REACH + z, REACH : REACH + rows, :] = zone_refs[1][f, z]
        low, high = REACH - 1, REACH + rows
        for pay, near, next_one, at in (
            (pay_refs[1], planes + REACH, planes + REACH + 1, total),
            (pay_refs[0], REACH - 1, REACH - 2, total + SUB),
        ):
            main[0][f, near, low - 1 : low + 1, :] = pay[f, at : at + 2, :]
            main[0][f, next_one, low : low + 1, :] = pay[f, at + 2 : at + 3, :]
            main[0][f, near, high : high + 2, :] = pay[f, at + 3 : at + 5, :]
            main[0][f, next_one, high : high + 1, :] = pay[f, at + 5 : at + 6, :]
        for t in range(tiles):
            cut = slice(SUB * t, SUB * (t + 1))
            before, after = pay_refs[0][f, cut, :], pay_refs[1][f, cut, :]
            span = WINDOW * REACH
            left = jnp.where(lane < span, turned(before, -WINDOW * planes), strips_ref[0, f, cut, :])
            strip[0][0, f, cut, :] = jnp.where(lane >= far, turned(after, far - span), left)
            right = jnp.where(lane < span, before, strips_ref[1, f, cut, :])
            strip[0][1, f, cut, :] = jnp.where(lane >= far, after, right)
    half = jnp.broadcast_to(0.5 * COURANT / jnp.max(top_ref[...], keepdims=True), (SUB, width))

    def x_pass(buffers, load, t):
        fx, gx, acc = buffers
        here, there = slice(SUB * t, SUB * (t + 1)), slice(SUB * t + 1, SUB * (t + 1) + 1)
        a, b = load(here), load(there)
        g = face(
            [fx[f, here, :] for f in range(5)],
            [fx[f, there, :] for f in range(5)],
            a,
            b,
            fx[5, here, :],
            fx[5, there, :],
        )
        for f in range(5):
            gx[f, SUB * (t + 1) : SUB * (t + 2), :] = g[f]
            below = gx[f, SUB * (t + 1) - 1 : SUB * (t + 2) - 1, :]
            acc[f, here, :] = acc[f, here, :] + (below - g[f])

    def keep_x(fx, state, ux, pressure, sound, cut):
        for f, v in enumerate(fluxes(state, ux, pressure, 1)):
            fx[f, cut, :] = v
        fx[5, cut, :] = jnp.abs(ux) + sound

    def strip_start(section, side, t):
        source, (fx, gx, acc) = strip[section], strip_buffers[side]
        cut = pl.ds(pl.multiple_of(SUB * t, SUB), SUB)
        state = [source[side, f, cut, :] for f in range(5)]
        ux, uy, uz, pressure, sound = primitives(*state)
        keep_x(fx, state, ux, pressure, sound, cut)
        change = along_y(state, fluxes(state, uy, pressure, 2), uy, pressure, jnp.abs(uy) + sound)
        signal = jnp.abs(uz) + sound
        other = [ahead(v, WINDOW) for v in state]
        g = face(
            fluxes(state, uz, pressure, 3),
            fluxes(other, ahead(uz, WINDOW), ahead(pressure, WINDOW), 3),
            state,
            other,
            signal,
            ahead(signal, WINDOW),
        )
        for f in range(5):
            acc[f, cut, :] = change[f] + (behind(g[f], WINDOW) - g[f])

    def strip_finish(section, side):
        source, target, buffers = strip[section], strip[section + 1], strip_buffers[side]
        for t in range(tiles):
            cut = slice(SUB * t, SUB * (t + 1))
            x_pass(buffers, lambda at: [source[side, f, at, :] for f in range(5)], t)
            for f in range(5):
                here, base = source[side, f, cut, :], strip[0][side, f, cut, :]
                target[side, f, cut, :] = blend(section, base, here, buffers[2][f, cut, :], half)

    def main_section(section, first, last):
        source, target, base = main[section], main[section + 1], main[0]

        def plane(w, with_face, with_finish, with_sides):
            def load(cut):
                return [source[f, w, cut, :] for f in range(5)]

            for t in range(tiles):
                cut = slice(SUB * t, SUB * (t + 1))
                state = load(cut)
                ux, uy, uz, pressure, sound = primitives(*state)
                flux, signal = fluxes(state, uz, pressure, 3), jnp.abs(uz) + sound
                if with_face:
                    before = [source[f, w - 1, cut, :] for f in range(5)]
                    flux_before = [fz[f, cut, :] for f in range(5)]
                    g = face(flux_before, flux, before, state, fz[5, cut, :], signal)
                    for f in range(5):
                        if with_finish:
                            change = acc[f, cut, :] + (gz[f, cut, :] - g[f])
                            started = base[f, w - 1, cut, :] if section else None
                            target[f, w - 1, cut, :] = blend(section, started, before[f], change, half)
                        if with_sides:
                            gz[f, cut, :] = g[f]
                if with_sides or not with_face:
                    for f in range(5):
                        fz[f, cut, :] = flux[f]
                    fz[5, cut, :] = signal
                if with_sides:
                    keep_x(fx, state, ux, pressure, sound, cut)
                    flux = fluxes(state, uy, pressure, 2)
                    change = along_y(state, flux, uy, pressure, jnp.abs(uy) + sound)
                    for f in range(5):
                        acc[f, cut, :] = change[f]
                    if t:
                        x_pass((fx, gx, acc), load, t - 1)
            if with_sides:
                x_pass((fx, gx, acc), load, tiles - 1)

        plane(first - 1, False, False, False)
        plane(first, True, False, True)

        count = last - first - 1
        for t in range(tiles - count):
            for side in range(2):
                strip_start(section, side, count + t)

        def step(w, carry):
            plane(w, True, True, True)
            for side in range(2):
                strip_start(section, side, jnp.minimum(w - first - 1, tiles - 1))
            return carry

        lax.fori_loop(first + 1, last, step, 0)
        plane(last, True, True, False)

    for section in range(3):
        main_section(section, 1 + section, planes + 2 * REACH - 1 - section)
        for side in range(2):
            strip_finish(section, side)
    column = lane % WINDOW
    for f in range(5):
        for t in range(rows // SUB):
            cut = slice(SUB * t + REACH, SUB * (t + 1) + REACH)
            edge = jnp.where(
                column < 2 * REACH, strip[3][1, f, cut, :], behind(strip[3][0, f, cut, :], REACH)
            )
            for z in range(planes):
                placed = turned(edge, width - REACH - (WINDOW * (z + REACH) + REACH))
                inner = main[3][f, z + REACH, cut, :]
                out_ref[f, z, SUB * t : SUB * (t + 1), :] = jnp.where(
                    (lane < REACH) | (lane >= width - REACH), placed, inner
                )
    for z in range(planes):
        state = [out_ref[f, z] for f in range(5)]
        rho_ref[z] = state[0]
        heat_ref[z] = primitives(*state)[3] / state[0]


def sections(wide, zones, pays, strips, top, rows):
    planes, total, width = wide.shape[1:]
    f32 = jnp.float32
    shared = len(zones) == 1
    tall, deep = total + SUB, planes + 2 * REACH
    args = [wide, *zones, *pays, strips, top]
    brick = jax.ShapeDtypeStruct((planes, rows, width), f32)
    return pl.pallas_call(
        functools.partial(section_kernel, shared),
        out_shape=[jax.ShapeDtypeStruct((5, planes, rows, width), f32), brick, brick],
        in_specs=[VMEM] * len(args),
        out_specs=[VMEM] * 3,
        scratch_shapes=[pltpu.VMEM((5, deep, tall, width), f32)] * 4
        + [pltpu.VMEM((2, 5, tall, width), f32)] * 4
        + [
            pltpu.VMEM((6, tall, width), f32),
            pltpu.VMEM((5, tall, width), f32),
            pltpu.VMEM((5, total, width), f32),
            pltpu.VMEM((6, total, width), f32),
            pltpu.VMEM((5, total, width), f32),
        ]
        + [
            pltpu.VMEM((6, tall, width), f32),
            pltpu.VMEM((5, tall, width), f32),
            pltpu.VMEM((5, total, width), f32),
        ]
        * 2,
        name="sections",
        compiler_params=grant(24),
    )(*args)


def lanes(values, index):
    return lax.gather(
        values,
        index[..., None],
        lax.GatherDimensionNumbers(
            offset_dims=(),
            collapsed_slice_dims=(1,),
            start_index_map=(1,),
            operand_batching_dims=(0,),
            start_indices_batching_dims=(0,),
        ),
        slice_sizes=(1, 1),
        mode=lax.GatherScatterMode.PROMISE_IN_BOUNDS,
    )


LEVELS = 65535
UNROLL = 4


def render_kernel(
    scale, begin, count, halves, rho_ref, heat_ref, palette_ref, index_ref, *refs
):
    outs, (table, ke, ko, we, wo, thick) = refs[: len(refs) - 6], refs[len(refs) - 6 :]
    planes, _, width = rho_ref.shape
    count_tf, bins = index_ref.shape
    half = bins // 2
    chosen = index_ref[...]
    if halves:
        swapped = pltpu.roll(chosen, count_tf // 2, axis=0)
        chosen = jnp.where(lax.axis_index("depth") == 0, swapped, chosen)
    colours = palette_ref[...]
    least = jnp.min(colours, keepdims=True)
    step = jnp.maximum(jnp.max(colours, keepdims=True) - least, 1e-6) * (1.0 / LEVELS)
    coded = ((colours - least) / step + 0.5).astype(jnp.int32)
    words = [(coded[c : c + 1] - (LEVELS + 1) // 2) * (LEVELS + 1) + coded[c + 1 : c + 2] for c in (0, 2)]
    lane = lax.broadcasted_iota(jnp.int32, (count_tf, half), 1)
    low, high = chosen[:, :half], chosen[:, half:]
    for parity in range(2):
        at = lane * 2 + parity
        inside = jnp.where(at < half, at, at - half)
        colour = jnp.where(at < half, lanes(low, inside), lanes(high, inside))
        wrapped = jnp.where(colour < half, colour, colour - half)
        for pair in range(2):
            first = jnp.broadcast_to(words[pair][:, :half], (count_tf, half))
            second = jnp.broadcast_to(words[pair][:, half:], (count_tf, half))
            table[pair, parity] = jnp.where(
                colour < half, lanes(first, wrapped), lanes(second, wrapped)
            )
    step_wide = jnp.broadcast_to(step, (SUB, width))
    for z in range(planes):
        for t in range(count // SUB):
            cut, from_cut = slice(SUB * t, SUB * (t + 1)), slice(begin + SUB * t, begin + SUB * (t + 1))
            rho = rho_ref[z, from_cut, :]
            position = jnp.clip(rho - 0.5, 0.0, 1.0) * (bins - 1)
            cell = jnp.minimum(position.astype(jnp.int32), bins - 2)
            even = (cell + 1) >> 1
            odd = cell >> 1
            ke[z, cut, :] = even
            ko[z, cut, :] = odd
            we[z, cut, :] = (1.0 - jnp.abs(position - (2 * even).astype(jnp.float32))) * step_wide
            wo[z, cut, :] = (1.0 - jnp.abs(position - (2 * odd + 1).astype(jnp.float32))) * step_wide
            thick[z, cut, :] = rho * (-scale * math.log2(math.e))
    tables = [[table[pair, p] for p in range(2)] for pair in range(2)]
    base_low = jnp.broadcast_to(least, (count_tf, width))
    base_high = base_low + jnp.broadcast_to(step, (count_tf, width)) * ((LEVELS + 1) // 2)

    def rays(group, carry):
        for i in range(UNROLL):
            ray(group * UNROLL + i)
        return carry

    def ray(x):
        trans = jnp.ones((count_tf, width), jnp.float32)
        light = [jnp.zeros((count_tf, width), jnp.float32) for _ in range(3)]
        for z in range(planes):

            def wide(ref, at=x):
                return jnp.broadcast_to(ref[z, pl.ds(at, 1), :], (count_tf, width))

            ie, io, fe, fo = wide(ke), wide(ko), wide(we), wide(wo)
            looked = []
            for pair in range(2):
                even, odd = lanes(tables[pair][0], ie), lanes(tables[pair][1], io)
                looked.append(
                    base_high
                    + (even >> 16).astype(jnp.float32) * fe
                    + (odd >> 16).astype(jnp.float32) * fo
                )
                looked.append(
                    base_low
                    + (even & LEVELS).astype(jnp.float32) * fe
                    + (odd & LEVELS).astype(jnp.float32) * fo
                )
            passed = trans * jnp.exp2(looked[3] * wide(thick))
            weight = (trans - passed) * wide(heat_ref, x + begin)
            light = [light[c] + looked[c] * weight for c in range(3)]
            trans = passed
        per_out = count_tf // len(outs)
        for c, values in enumerate(light + [trans]):
            for i, out in enumerate(outs):
                out[pl.ds(c * count + x, per_out, stride=4 * count), :] = values[
                    per_out * i : per_out * (i + 1)
                ]

    lax.fori_loop(0, count // UNROLL, rays, 0)


def render(rho, heat, palette, index, scale, begin, count, halves):
    planes, _, width = rho.shape
    count_tf, bins = index.shape
    parts = 2 if halves else 1
    per_out = count_tf // parts
    shape = jax.ShapeDtypeStruct((per_out * 4 * count, width), jnp.float32)
    scratch = [pltpu.VMEM((planes, count, width), t) for t in (jnp.int32,) * 2 + (jnp.float32,) * 3]
    outs = pl.pallas_call(
        functools.partial(render_kernel, scale, begin, count, halves),
        out_shape=[shape] * parts,
        in_specs=[VMEM] * 4,
        out_specs=[VMEM] * parts,
        scratch_shapes=[pltpu.VMEM((2, 2, count_tf, bins // 2), jnp.int32)] + scratch,
        compiler_params=grant(8),
    )(rho, heat, palette, index)
    return [out.reshape(per_out, 4, count, width) for out in outs]


def exchange_max(value, axis, step):
    size = lax.axis_size(axis)
    if size & (size - 1) == 0:
        route = [(i, i ^ step) for i in range(size)]
    else:
        route = along(axis, step, True)
    return jnp.maximum(value, lax.ppermute(value, axis, route))


def largest(value, axis, step=1):
    while step < lax.axis_size(axis):
        value = exchange_max(value, axis, step)
        step *= 2
    return value


def composed(shares):
    light, passed = None, None
    for d in range(shares.shape[0]):
        slab = shares[d]
        light = slab[:, :3] if d == 0 else light + passed * slab[:, :3]
        passed = slab[:, 3:] if d == 0 else passed * slab[:, 3:]
    return light


def along(axis, distance, wrap):
    size = lax.axis_size(axis)
    if wrap:
        return [(i, (i + distance) % size) for i in range(size)]
    return [(i, i + distance) for i in range(size) if 0 <= i + distance < size]


def pictured(rho, heat, palette, index):
    depth = lax.axis_size("depth")
    planes, rows, _ = rho.shape
    scale = 2.0 / (planes * depth)
    if depth != 2:
        (shares,) = render(rho, heat, palette, index, scale, 0, rows, False)
        parts = shares.reshape((depth, shares.shape[0] // depth) + shares.shape[1:])
        return composed(lax.all_to_all(parts, "depth", 0, 0, tiled=True))
    pieces = PIECES if rows % (PIECES * SUB) == 0 else 1
    chunk = rows // pieces
    kept, sent = [], []
    for i in range(pieces):
        other, own = render(rho, heat, palette, index, scale, i * chunk, chunk, True)
        kept.append(own)
        sent.append(lax.ppermute(other, "depth", along("depth", 1, True)))
    in_front = lax.axis_index("depth") == 0
    shown = []
    for own, other in zip(kept, sent):
        front, back = jnp.where(in_front, own, other), jnp.where(in_front, other, own)
        shown.append(front[:, :3] + front[:, 3:] * back[:, :3])
    return jnp.concatenate(shown, axis=2)


def whole_step(density, velocity, pressure, palette, palette_index):
    depth = lax.axis_size("depth")
    _, rows = density.shape[:2]
    state, zone, low, high, top = opening(density, velocity, pressure)

    def both_ways(block):
        if depth == 2:
            return (lax.ppermute(block, "depth", along("depth", 1, True)),)
        return tuple(lax.ppermute(block, "depth", along("depth", d, True)) for d in (1, -1))

    from_below = lax.ppermute(high, "group", along("group", 1, False))
    from_above = lax.ppermute(low, "group", along("group", -1, False))
    zones = both_ways(zone)
    wide, right, left, top = windows(state, from_below, from_above, top)
    from_right = lax.ppermute(right, "image", along("image", -1, True))
    from_left = lax.ppermute(left, "image", along("image", 1, True))
    if lax.axis_size("group") == 4:
        top = exchange_max(top, "group", 2)
    else:
        top = largest(top, "group")
    top = exchange_max(top, "image", 1)
    from_right, from_left, top = lax.optimization_barrier((from_right, from_left, top))
    strips, pay = strips_of(wide, right, left, from_right, from_left)
    pays = both_ways(pay)
    top = largest(largest(top, "image", 2), "depth")
    fluid_state, rho, heat = sections(wide, zones, pays, strips, top, rows)
    return (fluid_state, pictured(rho, heat, palette, palette_index))


def solution(mesh):
    return jax.shard_map(
        whole_step,
        mesh=mesh,
        in_specs=(
            P("depth", "group", "image"),
            P(None, "depth", "group", "image"),
            P("depth", "group", "image"),
            P(),
            P(),
        ),
        out_specs=(P(None, "depth", "group", "image"), P("depth", None, "group", "image")),
        check_vma=False,
    )
```

```python
import functools
import math

import jax
import jax.numpy as jnp
from jax import lax
from jax.experimental import pallas as pl
from jax.experimental.pallas import tpu as pltpu
from jax.sharding import PartitionSpec as P


HEAT_RATIO = 1.4
COURANT = 0.8
REACH = 3
WINDOW = 3 * REACH
SUB = 8
PIECES = 3
VMEM = pl.BlockSpec(memory_space=pltpu.VMEM)
MIB = 1 << 20


def grant(mib):
    return pltpu.CompilerParams(vmem_limit_bytes=mib * MIB)


def ahead(values, distance=1):
    return pltpu.roll(values, values.shape[-1] - distance, axis=values.ndim - 1)


def behind(values, distance=1):
    return pltpu.roll(values, distance, axis=values.ndim - 1)


def turned(values, shift):
    return pltpu.roll(values, shift % values.shape[-1], axis=values.ndim - 1)


def padded_rows(rows):
    return -(-(rows + 2 * REACH) // SUB) * SUB


def primitives(rho, mx, my, mz, energy):
    inverse = 1.0 / rho
    ux, uy, uz = mx * inverse, my * inverse, mz * inverse
    pressure = (HEAT_RATIO - 1.0) * (energy - 0.5 * (mx * ux + my * uy + mz * uz))
    sound = jnp.sqrt(HEAT_RATIO * pressure * inverse)
    return ux, uy, uz, pressure, sound


def fluxes(state, normal, pressure, component):
    _, mx, my, mz, energy = state
    rows = [state[component], mx * normal, my * normal, mz * normal, (energy + pressure) * normal]
    rows[component] = rows[component] + pressure
    return rows


def face(flux_a, flux_b, state_a, state_b, signal_a, signal_b):
    fastest = jnp.maximum(signal_a, signal_b)
    return [
        (fa + fb) - fastest * (ub - ua)
        for fa, fb, ua, ub in zip(flux_a, flux_b, state_a, state_b)
    ]


def opening_kernel(
    rho_hbm, vel_hbm, pre_hbm, state_ref, zpay_ref, one_ref, two_ref, top_ref, rho_ref, vel_ref, pre_ref, sems
):
    planes, rows, width = rho_ref.shape
    pairs = ((rho_hbm, rho_ref), (vel_hbm, vel_ref), (pre_hbm, pre_ref))
    copies = [pltpu.make_async_copy(src, dst, sems.at[i]) for i, (src, dst) in enumerate(pairs)]
    for copy in copies:
        copy.start()
    for copy in copies:
        copy.wait()
    even = (lax.axis_index("group") & 1) == 0
    edge = list(range(REACH)) + list(range(planes - REACH, planes))
    fastest = None
    for z in range(planes):
        rho, p = rho_ref[z], pre_ref[z]
        v = [vel_ref[i, z] for i in range(3)]
        signal = jnp.abs(v[0]) + jnp.abs(v[1]) + jnp.abs(v[2]) + 3.0 * jnp.sqrt(HEAT_RATIO * p / rho)
        signal = jnp.max(signal.reshape(rows // SUB, SUB, width), axis=0)
        fastest = signal if fastest is None else jnp.maximum(fastest, signal)
        kinetic = 0.5 * rho * (v[0] * v[0] + v[1] * v[1] + v[2] * v[2])
        fields = [rho, rho * v[0], rho * v[1], rho * v[2], p / (HEAT_RATIO - 1.0) + kinetic]
        for f in range(5):
            state_ref[f, z] = fields[f]
            if z in edge:
                zpay_ref[f, edge.index(z)] = fields[f]
            at = (f * planes + z) * REACH
            low, high = fields[f][:REACH], fields[f][rows - REACH :]
            one_ref[at : at + REACH, :] = jnp.where(even, high, low)
            two_ref[at : at + REACH, :] = jnp.where(even, low, high)
    top_ref[...] = fastest
    for ref in (one_ref, two_ref):
        ref[5 * planes * REACH :, :] = fastest


def opening(density, velocity, pressure):
    planes, rows, width = density.shape
    f32 = jnp.float32
    return pl.pallas_call(
        opening_kernel,
        out_shape=[
            jax.ShapeDtypeStruct((5, planes, rows, width), f32),
            jax.ShapeDtypeStruct((5, 2 * REACH, rows, width), f32),
            jax.ShapeDtypeStruct((5 * planes * REACH + SUB, width), f32),
            jax.ShapeDtypeStruct((5 * planes * REACH + SUB, width), f32),
            jax.ShapeDtypeStruct((SUB, width), f32),
        ],
        in_specs=[pl.BlockSpec(memory_space=pltpu.HBM)] * 3,
        out_specs=[VMEM] * 5,
        scratch_shapes=[
            pltpu.VMEM(density.shape, f32),
            pltpu.VMEM(velocity.shape, f32),
            pltpu.VMEM(pressure.shape, f32),
            pltpu.SemaphoreType.DMA((3,)),
        ],
        name="opening",
        compiler_params=grant(8),
    )(*[pltpu.with_memory_space_constraint(a, pltpu.HBM) for a in (density, velocity, pressure)])


def window_kernel(
    state_ref, one_ref, two_ref, top_ref, wide_ref, first_ref, second_ref, peak_ref
):
    planes, rows, width = state_ref.shape[1:]
    sent = slice(5 * planes * REACH, 5 * planes * REACH + SUB)
    peak_ref[...] = jnp.maximum(top_ref[...], jnp.maximum(one_ref[sent, :], two_ref[sent, :]))
    total = wide_ref.shape[2]
    group, groups = lax.axis_index("group"), lax.axis_size("group")
    even, even_image = (group & 1) == 0, (lax.axis_index("image") & 1) == 0
    lane = lax.broadcasted_iota(jnp.int32, (SUB, width), 1)
    for f in range(5):
        sign = -1.0 if f == 1 else 1.0
        for z in range(planes):
            at = (f * planes + z) * REACH
            wide_ref[f, z, REACH : REACH + rows, :] = state_ref[f, z]
            mirrored = [state_ref[f, z, r : r + 1, :] * sign for r in range(REACH - 1, -1, -1)]
            one, two = one_ref[at : at + REACH, :], two_ref[at : at + REACH, :]
            below = jnp.where(
                group == 0, jnp.concatenate(mirrored, axis=0), jnp.where(even, two, one)
            )
            wide_ref[f, z, :REACH, :] = below
            mirrored = [state_ref[f, z, rows - 1 - r : rows - r, :] * sign for r in range(REACH)]
            above = jnp.where(
                group == groups - 1, jnp.concatenate(mirrored, axis=0), jnp.where(even, one, two)
            )
            wide_ref[f, z, REACH + rows : 2 * REACH + rows, :] = above

    def fields(f, carry):
        for t in range(total // SUB):
            cut = slice(SUB * t, SUB * (t + 1))
            right = jnp.zeros((SUB, width), jnp.float32)
            left = right
            for z in range(planes):
                start = WINDOW * (z + REACH)
                inside = (lane >= start) & (lane < start + WINDOW)
                values = wide_ref[f, z, cut, :]
                right = jnp.where(inside, turned(values, start - (width - 2 * REACH)), right)
                left = jnp.where(inside, turned(values, start - (width - REACH)), left)
            first_ref[f, cut, :] = jnp.where(even_image, left, right)
            second_ref[f, cut, :] = jnp.where(even_image, right, left)
        return carry

    lax.fori_loop(0, 5, fields, 0)


def windows(state, one, two, top):
    planes, rows, width = state.shape[1:]
    total = padded_rows(rows)
    f32 = jnp.float32
    return pl.pallas_call(
        window_kernel,
        out_shape=[
            jax.ShapeDtypeStruct((5, planes, total, width), f32),
            jax.ShapeDtypeStruct((5, total, width), f32),
            jax.ShapeDtypeStruct((5, total, width), f32),
            jax.ShapeDtypeStruct((SUB, width), f32),
        ],
        in_specs=[VMEM] * 4,
        out_specs=[VMEM] * 4,
        name="windows",
        compiler_params=grant(8),
    )(state, one, two, top)


def strip_kernel(wide_ref, first_ref, second_ref, got_first, got_second, strips_ref, pay_ref):
    even = (lax.axis_index("image") & 1) == 0
    planes, total, width = wide_ref.shape[1:]
    rows = total - 2 * REACH - (total - 2 * REACH) % SUB
    lane = lax.broadcasted_iota(jnp.int32, (SUB, width), 1)
    column = lane % WINDOW
    span = WINDOW * REACH
    start, last = WINDOW * REACH, WINDOW * planes
    far = WINDOW * (REACH + planes)
    for f in range(5):
        for t in range(total // SUB):
            cut = slice(SUB * t, SUB * (t + 1))
            first, second = first_ref[f, cut, :], second_ref[f, cut, :]
            near, after = got_first[f, cut, :], got_second[f, cut, :]
            right = jnp.where(
                column >= 2 * REACH, jnp.where(even, near, after), jnp.where(even, second, first)
            )
            left = jnp.where(
                column < REACH, jnp.where(even, after, near), jnp.where(even, first, second)
            )
            strips_ref[0, f, cut, :] = left
            strips_ref[1, f, cut, :] = right
            sent = jnp.where(lane < span, turned(right, -last), left)
            pay_ref[f, cut, :] = jnp.where(lane >= far, turned(right, far - start), sent)
        low, high = REACH - 1, REACH + rows
        for side, (near, next_one) in enumerate(((0, 1), (planes - 1, planes - 2))):
            at = total + SUB * side
            pay_ref[f, at : at + 2, :] = wide_ref[f, near, low - 1 : low + 1, :]
            pay_ref[f, at + 2 : at + 3, :] = wide_ref[f, next_one, low : low + 1, :]
            pay_ref[f, at + 3 : at + 5, :] = wide_ref[f, near, high : high + 2, :]
            pay_ref[f, at + 5 : at + 6, :] = wide_ref[f, next_one, high : high + 1, :]
            pay_ref[f, at + 6 : at + 8, :] = jnp.zeros((2, width), jnp.float32)


def strips_of(wide, first, second, got_first, got_second):
    _, total, width = wide.shape[1:]
    f32 = jnp.float32
    return pl.pallas_call(
        strip_kernel,
        out_shape=[
            jax.ShapeDtypeStruct((2, 5, total, width), f32),
            jax.ShapeDtypeStruct((5, total + 2 * SUB, width), f32),
        ],
        in_specs=[VMEM] * 5,
        out_specs=[VMEM] * 2,
        name="strips",
        compiler_params=grant(8),
    )(wide, first, second, got_first, got_second)


def blend(section, base, here, change, half):
    if section == 0:
        return here + half * change
    if section == 1:
        return 0.75 * base + 0.25 * (here + half * change)
    return base * (1.0 / 3.0) + (2.0 / 3.0) * (here + half * change)


def along_y(state, flux, uy, pressure, signal):
    other = [ahead(v) for v in state]
    flux_other = fluxes(other, ahead(uy), ahead(pressure), 2)
    g = face(flux, flux_other, state, other, signal, ahead(signal))
    return [behind(v) - v for v in g]


def section_kernel(shared, *refs):
    if shared:
        wide_ref, zone_ref, pay_ref, strips_ref, top_ref = refs[:5]
        zone_refs, pay_refs = (zone_ref, zone_ref), (pay_ref, pay_ref)
        rest = refs[5:]
    else:
        wide_ref, strips_ref, top_ref = refs[0], refs[5], refs[6]
        zone_refs, pay_refs = refs[1:3], refs[3:5]
        rest = refs[7:]
    out_ref, rho_ref, heat_ref = rest[:3]
    main, strip, (fx, gx, acc, fz, gz) = rest[3:7], rest[7:11], rest[11:16]
    strip_buffers = (rest[16:19], rest[19:22])
    planes, total, width = wide_ref.shape[1:]
    rows = out_ref.shape[2]
    tiles = total // SUB
    lane = lax.broadcasted_iota(jnp.int32, (SUB, width), 1)
    far = WINDOW * (REACH + planes)
    for f in range(5):
        for z in range(planes):
            main[0][f, z + REACH, :total, :] = wide_ref[f, z]
        for z in range(REACH):
            main[0][f, z, REACH : REACH + rows, :] = zone_refs[0][f, REACH + z]
            main[0][f, planes + REACH + z, REACH : REACH + rows, :] = zone_refs[1][f, z]
        low, high = REACH - 1, REACH + rows
        for pay, near, next_one, at in (
            (pay_refs[1], planes + REACH, planes + REACH + 1, total),
            (pay_refs[0], REACH - 1, REACH - 2, total + SUB),
        ):
            main[0][f, near, low - 1 : low + 1, :] = pay[f, at : at + 2, :]
            main[0][f, next_one, low : low + 1, :] = pay[f, at + 2 : at + 3, :]
            main[0][f, near, high : high + 2, :] = pay[f, at + 3 : at + 5, :]
            main[0][f, next_one, high : high + 1, :] = pay[f, at + 5 : at + 6, :]
        for t in range(tiles):
            cut = slice(SUB * t, SUB * (t + 1))
            before, after = pay_refs[0][f, cut, :], pay_refs[1][f, cut, :]
            span = WINDOW * REACH
            left = jnp.where(lane < span, turned(before, -WINDOW * planes), strips_ref[0, f, cut, :])
            strip[0][0, f, cut, :] = jnp.where(lane >= far, turned(after, far - span), left)
            right = jnp.where(lane < span, before, strips_ref[1, f, cut, :])
            strip[0][1, f, cut, :] = jnp.where(lane >= far, after, right)
    half = jnp.broadcast_to(0.5 * COURANT / jnp.max(top_ref[...], keepdims=True), (SUB, width))

    def x_pass(buffers, load, t):
        fx, gx, acc = buffers
        here, there = slice(SUB * t, SUB * (t + 1)), slice(SUB * t + 1, SUB * (t + 1) + 1)
        a, b = load(here), load(there)
        g = face(
            [fx[f, here, :] for f in range(5)],
            [fx[f, there, :] for f in range(5)],
            a,
            b,
            fx[5, here, :],
            fx[5, there, :],
        )
        for f in range(5):
            gx[f, SUB * (t + 1) : SUB * (t + 2), :] = g[f]
            below = gx[f, SUB * (t + 1) - 1 : SUB * (t + 2) - 1, :]
            acc[f, here, :] = acc[f, here, :] + (below - g[f])

    def keep_x(fx, state, ux, pressure, sound, cut):
        for f, v in enumerate(fluxes(state, ux, pressure, 1)):
            fx[f, cut, :] = v
        fx[5, cut, :] = jnp.abs(ux) + sound

    def strip_start(section, side, t):
        source, (fx, gx, acc) = strip[section], strip_buffers[side]
        cut = pl.ds(pl.multiple_of(SUB * t, SUB), SUB)
        state = [source[side, f, cut, :] for f in range(5)]
        ux, uy, uz, pressure, sound = primitives(*state)
        keep_x(fx, state, ux, pressure, sound, cut)
        change = along_y(state, fluxes(state, uy, pressure, 2), uy, pressure, jnp.abs(uy) + sound)
        signal = jnp.abs(uz) + sound
        other = [ahead(v, WINDOW) for v in state]
        g = face(
            fluxes(state, uz, pressure, 3),
            fluxes(other, ahead(uz, WINDOW), ahead(pressure, WINDOW), 3),
            state,
            other,
            signal,
            ahead(signal, WINDOW),
        )
        for f in range(5):
            acc[f, cut, :] = change[f] + (behind(g[f], WINDOW) - g[f])

    def strip_finish(section, side):
        source, target, buffers = strip[section], strip[section + 1], strip_buffers[side]
        for t in range(tiles):
            cut = slice(SUB * t, SUB * (t + 1))
            x_pass(buffers, lambda at: [source[side, f, at, :] for f in range(5)], t)
            for f in range(5):
                here, base = source[side, f, cut, :], strip[0][side, f, cut, :]
                target[side, f, cut, :] = blend(section, base, here, buffers[2][f, cut, :], half)

    def main_section(section, first, last):
        source, target, base = main[section], main[section + 1], main[0]

        def plane(w, with_face, with_finish, with_sides):
            def load(cut):
                return [source[f, w, cut, :] for f in range(5)]

            for t in range(tiles):
                cut = slice(SUB * t, SUB * (t + 1))
                state = load(cut)
                ux, uy, uz, pressure, sound = primitives(*state)
                flux, signal = fluxes(state, uz, pressure, 3), jnp.abs(uz) + sound
                if with_face:
                    before = [source[f, w - 1, cut, :] for f in range(5)]
                    flux_before = [fz[f, cut, :] for f in range(5)]
                    g = face(flux_before, flux, before, state, fz[5, cut, :], signal)
                    for f in range(5):
                        if with_finish:
                            change = acc[f, cut, :] + (gz[f, cut, :] - g[f])
                            started = base[f, w - 1, cut, :] if section else None
                            target[f, w - 1, cut, :] = blend(section, started, before[f], change, half)
                        if with_sides:
                            gz[f, cut, :] = g[f]
                if with_sides or not with_face:
                    for f in range(5):
                        fz[f, cut, :] = flux[f]
                    fz[5, cut, :] = signal
                if with_sides:
                    keep_x(fx, state, ux, pressure, sound, cut)
                    flux = fluxes(state, uy, pressure, 2)
                    change = along_y(state, flux, uy, pressure, jnp.abs(uy) + sound)
                    for f in range(5):
                        acc[f, cut, :] = change[f]
                    if t:
                        x_pass((fx, gx, acc), load, t - 1)
            if with_sides:
                x_pass((fx, gx, acc), load, tiles - 1)

        plane(first - 1, False, False, False)
        plane(first, True, False, True)

        count = last - first - 1
        for t in range(tiles - count):
            for side in range(2):
                strip_start(section, side, count + t)

        def step(w, carry):
            plane(w, True, True, True)
            for side in range(2):
                strip_start(section, side, jnp.minimum(w - first - 1, tiles - 1))
            return carry

        lax.fori_loop(first + 1, last, step, 0)
        plane(last, True, True, False)

    for section in range(3):
        main_section(section, 1 + section, planes + 2 * REACH - 1 - section)
        for side in range(2):
            strip_finish(section, side)
    column = lane % WINDOW
    for f in range(5):
        for t in range(rows // SUB):
            cut = slice(SUB * t + REACH, SUB * (t + 1) + REACH)
            edge = jnp.where(
                column < 2 * REACH, strip[3][1, f, cut, :], behind(strip[3][0, f, cut, :], REACH)
            )
            for z in range(planes):
                placed = turned(edge, width - REACH - (WINDOW * (z + REACH) + REACH))
                inner = main[3][f, z + REACH, cut, :]
                out_ref[f, z, SUB * t : SUB * (t + 1), :] = jnp.where(
                    (lane < REACH) | (lane >= width - REACH), placed, inner
                )
    for z in range(planes):
        state = [out_ref[f, z] for f in range(5)]
        rho_ref[z] = state[0]
        heat_ref[z] = primitives(*state)[3] / state[0]


def sections(wide, zones, pays, strips, top, rows):
    planes, total, width = wide.shape[1:]
    f32 = jnp.float32
    shared = len(zones) == 1
    tall, deep = total + SUB, planes + 2 * REACH
    args = [wide, *zones, *pays, strips, top]
    brick = jax.ShapeDtypeStruct((planes, rows, width), f32)
    return pl.pallas_call(
        functools.partial(section_kernel, shared),
        out_shape=[pltpu.VMEM((5, planes, rows, width), f32), brick, brick],
        in_specs=[VMEM] * len(args),
        out_specs=[VMEM] * 3,
        scratch_shapes=[pltpu.VMEM((5, deep, tall, width), f32)] * 4
        + [pltpu.VMEM((2, 5, tall, width), f32)] * 4
        + [
            pltpu.VMEM((6, tall, width), f32),
            pltpu.VMEM((5, tall, width), f32),
            pltpu.VMEM((5, total, width), f32),
            pltpu.VMEM((6, total, width), f32),
            pltpu.VMEM((5, total, width), f32),
        ]
        + [
            pltpu.VMEM((6, tall, width), f32),
            pltpu.VMEM((5, tall, width), f32),
            pltpu.VMEM((5, total, width), f32),
        ]
        * 2,
        name="sections",
        compiler_params=grant(24),
    )(*args)


def lanes(values, index):
    return lax.gather(
        values,
        index[..., None],
        lax.GatherDimensionNumbers(
            offset_dims=(),
            collapsed_slice_dims=(1,),
            start_index_map=(1,),
            operand_batching_dims=(0,),
            start_indices_batching_dims=(0,),
        ),
        slice_sizes=(1, 1),
        mode=lax.GatherScatterMode.PROMISE_IN_BOUNDS,
    )


LEVELS = 65535
UNROLL = 4


def render_kernel(
    scale, begin, count, halves, rho_ref, heat_ref, palette_ref, index_ref, *refs
):
    outs, (table, ke, ko, we, wo, thick) = refs[: len(refs) - 6], refs[len(refs) - 6 :]
    planes, _, width = rho_ref.shape
    count_tf, bins = index_ref.shape
    half = bins // 2
    chosen = index_ref[...]
    if halves:
        swapped = pltpu.roll(chosen, count_tf // 2, axis=0)
        chosen = jnp.where(lax.axis_index("depth") == 0, swapped, chosen)
    colours = palette_ref[...]
    least = jnp.min(colours, keepdims=True)
    step = jnp.maximum(jnp.max(colours, keepdims=True) - least, 1e-6) * (1.0 / LEVELS)
    coded = ((colours - least) / step + 0.5).astype(jnp.int32)
    words = [(coded[c : c + 1] - (LEVELS + 1) // 2) * (LEVELS + 1) + coded[c + 1 : c + 2] for c in (0, 2)]
    lane = lax.broadcasted_iota(jnp.int32, (count_tf, half), 1)
    low, high = chosen[:, :half], chosen[:, half:]
    for parity in range(2):
        at = lane * 2 + parity
        inside = jnp.where(at < half, at, at - half)
        colour = jnp.where(at < half, lanes(low, inside), lanes(high, inside))
        wrapped = jnp.where(colour < half, colour, colour - half)
        for pair in range(2):
            first = jnp.broadcast_to(words[pair][:, :half], (count_tf, half))
            second = jnp.broadcast_to(words[pair][:, half:], (count_tf, half))
            table[pair, parity] = jnp.where(
                colour < half, lanes(first, wrapped), lanes(second, wrapped)
            )
    step_wide = jnp.broadcast_to(step, (SUB, width))
    for z in range(planes):
        for t in range(count // SUB):
            cut, from_cut = slice(SUB * t, SUB * (t + 1)), slice(begin + SUB * t, begin + SUB * (t + 1))
            rho = rho_ref[z, from_cut, :]
            position = jnp.clip(rho - 0.5, 0.0, 1.0) * (bins - 1)
            cell = jnp.minimum(position.astype(jnp.int32), bins - 2)
            even = (cell + 1) >> 1
            odd = cell >> 1
            ke[z, cut, :] = even
            ko[z, cut, :] = odd
            we[z, cut, :] = (1.0 - jnp.abs(position - (2 * even).astype(jnp.float32))) * step_wide
            wo[z, cut, :] = (1.0 - jnp.abs(position - (2 * odd + 1).astype(jnp.float32))) * step_wide
            thick[z, cut, :] = rho * (-scale * math.log2(math.e))
    tables = [[table[pair, p] for p in range(2)] for pair in range(2)]
    base_low = jnp.broadcast_to(least, (count_tf, width))
    base_high = base_low + jnp.broadcast_to(step, (count_tf, width)) * ((LEVELS + 1) // 2)

    def rays(group, carry):
        for i in range(UNROLL):
            ray(group * UNROLL + i)
        return carry

    def ray(x):
        trans = jnp.ones((count_tf, width), jnp.float32)
        light = [jnp.zeros((count_tf, width), jnp.float32) for _ in range(3)]
        for z in range(planes):

            def wide(ref, at=x):
                return jnp.broadcast_to(ref[z, pl.ds(at, 1), :], (count_tf, width))

            ie, io, fe, fo = wide(ke), wide(ko), wide(we), wide(wo)
            looked = []
            for pair in range(2):
                even, odd = lanes(tables[pair][0], ie), lanes(tables[pair][1], io)
                looked.append(
                    base_high
                    + (even >> 16).astype(jnp.float32) * fe
                    + (odd >> 16).astype(jnp.float32) * fo
                )
                looked.append(
                    base_low
                    + (even & LEVELS).astype(jnp.float32) * fe
                    + (odd & LEVELS).astype(jnp.float32) * fo
                )
            passed = trans * jnp.exp2(looked[3] * wide(thick))
            weight = (trans - passed) * wide(heat_ref, x + begin)
            light = [light[c] + looked[c] * weight for c in range(3)]
            trans = passed
        per_out = count_tf // len(outs)
        for c, values in enumerate(light + [trans]):
            for i, out in enumerate(outs):
                out[pl.ds(c * count + x, per_out, stride=4 * count), :] = values[
                    per_out * i : per_out * (i + 1)
                ]

    lax.fori_loop(0, count // UNROLL, rays, 0)


def render(rho, heat, palette, index, scale, begin, count, halves):
    planes, _, width = rho.shape
    count_tf, bins = index.shape
    parts = 2 if halves else 1
    per_out = count_tf // parts
    shape = jax.ShapeDtypeStruct((per_out * 4 * count, width), jnp.float32)
    scratch = [pltpu.VMEM((planes, count, width), t) for t in (jnp.int32,) * 2 + (jnp.float32,) * 3]
    outs = pl.pallas_call(
        functools.partial(render_kernel, scale, begin, count, halves),
        out_shape=[shape] * parts,
        in_specs=[VMEM] * 4,
        out_specs=[VMEM] * parts,
        scratch_shapes=[pltpu.VMEM((2, 2, count_tf, bins // 2), jnp.int32)] + scratch,
        compiler_params=grant(8),
    )(rho, heat, palette, index)
    return [out.reshape(per_out, 4, count, width) for out in outs]


def exchange_max(value, axis, step):
    size = lax.axis_size(axis)
    if size & (size - 1) == 0:
        route = [(i, i ^ step) for i in range(size)]
    else:
        route = along(axis, step, True)
    return jnp.maximum(value, lax.ppermute(value, axis, route))


def last_rounds(value):
    images, depth = lax.axis_size("image"), lax.axis_size("depth")
    if images != 4 or depth != 2:
        return largest(largest(value, "image", 2), "depth")
    others = []
    for flip_depth, flip_image in ((1, 0), (0, 2), (1, 2)):
        route = [
            (d * images + i, (d ^ flip_depth) * images + (i ^ flip_image))
            for d in range(depth)
            for i in range(images)
        ]
        others.append(lax.ppermute(value, ("depth", "image"), route))
    for other in others:
        value = jnp.maximum(value, other)
    return value


def largest(value, axis, step=1):
    while step < lax.axis_size(axis):
        value = exchange_max(value, axis, step)
        step *= 2
    return value


def composed(shares):
    light, passed = None, None
    for d in range(shares.shape[0]):
        slab = shares[d]
        light = slab[:, :3] if d == 0 else light + passed * slab[:, :3]
        passed = slab[:, 3:] if d == 0 else passed * slab[:, 3:]
    return light


def along(axis, distance, wrap):
    size = lax.axis_size(axis)
    if wrap:
        return [(i, (i + distance) % size) for i in range(size)]
    return [(i, i + distance) for i in range(size) if 0 <= i + distance < size]


def paired(axis, start, wrap):
    size = lax.axis_size(axis)
    assert not wrap or size % 2 == 0, "odd ring"
    couples = [(i, (i + 1) % size) for i in range(start, size, 2) if wrap or i + 1 < size]
    return couples + [(j, i) for i, j in couples]


def pictured(rho, heat, palette, index):
    depth = lax.axis_size("depth")
    planes, rows, _ = rho.shape
    scale = 2.0 / (planes * depth)
    if depth != 2:
        (shares,) = render(rho, heat, palette, index, scale, 0, rows, False)
        parts = shares.reshape((depth, shares.shape[0] // depth) + shares.shape[1:])
        return composed(lax.all_to_all(parts, "depth", 0, 0, tiled=True))
    pieces = PIECES if rows % (PIECES * SUB) == 0 else 1
    chunk = rows // pieces
    kept, sent = [], []
    for i in range(pieces):
        other, own = render(rho, heat, palette, index, scale, i * chunk, chunk, True)
        kept.append(own)
        sent.append(lax.ppermute(other, "depth", along("depth", 1, True)))
    in_front = lax.axis_index("depth") == 0
    shown = []
    for own, other in zip(kept, sent):
        front, back = jnp.where(in_front, own, other), jnp.where(in_front, other, own)
        shown.append(front[:, :3] + front[:, 3:] * back[:, :3])
    return jnp.concatenate(shown, axis=2)


def whole_step(density, velocity, pressure, palette, palette_index):
    depth = lax.axis_size("depth")
    _, rows = density.shape[:2]
    state, zone, one, two, top = opening(density, velocity, pressure)

    def both_ways(block):
        if depth == 2:
            return (lax.ppermute(block, "depth", along("depth", 1, True)),)
        return tuple(lax.ppermute(block, "depth", along("depth", d, True)) for d in (1, -1))

    got_one = lax.ppermute(one, "group", paired("group", 0, False))
    got_two = lax.ppermute(two, "group", paired("group", 1, False))
    zones = both_ways(zone)
    wide, first, second, top = windows(state, got_one, got_two, top)
    got_first = lax.ppermute(first, "image", paired("image", 0, True))
    got_second = lax.ppermute(second, "image", paired("image", 1, True))
    if lax.axis_size("group") == 4:
        top = exchange_max(top, "group", 2)
    else:
        top = largest(top, "group")
    top = exchange_max(top, "image", 1)
    got_first, got_second, top = lax.optimization_barrier((got_first, got_second, top))
    strips, pay = strips_of(wide, first, second, got_first, got_second)
    pays = both_ways(pay)
    top = last_rounds(top)
    fluid_state, rho, heat = sections(wide, zones, pays, strips, top, rows)
    return (fluid_state, pictured(rho, heat, palette, palette_index))


def solution(mesh):
    return jax.shard_map(
        whole_step,
        mesh=mesh,
        in_specs=(
            P("depth", "group", "image"),
            P(None, "depth", "group", "image"),
            P("depth", "group", "image"),
            P(),
            P(),
        ),
        out_specs=(P(None, "depth", "group", "image"), P("depth", None, "group", "image")),
        check_vma=False,
    )
```

```python
import functools
import math

import jax
import jax.numpy as jnp
from jax import lax
from jax.experimental import pallas as pl
from jax.experimental.pallas import tpu as pltpu
from jax.sharding import PartitionSpec as P


HEAT_RATIO = 1.4
COURANT = 0.8
REACH = 3
WINDOW = 3 * REACH
SUB = 8
PIECES = 3
VMEM = pl.BlockSpec(memory_space=pltpu.VMEM)
MIB = 1 << 20


def grant(mib):
    return pltpu.CompilerParams(vmem_limit_bytes=mib * MIB)


def ahead(values, distance=1):
    return pltpu.roll(values, values.shape[-1] - distance, axis=values.ndim - 1)


def behind(values, distance=1):
    return pltpu.roll(values, distance, axis=values.ndim - 1)


def turned(values, shift):
    return pltpu.roll(values, shift % values.shape[-1], axis=values.ndim - 1)


def padded_rows(rows):
    return -(-(rows + 2 * REACH) // SUB) * SUB


def primitives(rho, mx, my, mz, energy):
    inverse = 1.0 / rho
    ux, uy, uz = mx * inverse, my * inverse, mz * inverse
    pressure = (HEAT_RATIO - 1.0) * (energy - 0.5 * (mx * ux + my * uy + mz * uz))
    sound = jnp.sqrt(HEAT_RATIO * pressure * inverse)
    return ux, uy, uz, pressure, sound


def fluxes(state, normal, pressure, component):
    _, mx, my, mz, energy = state
    rows = [state[component], mx * normal, my * normal, mz * normal, (energy + pressure) * normal]
    rows[component] = rows[component] + pressure
    return rows


def face(flux_a, flux_b, state_a, state_b, signal_a, signal_b):
    fastest = jnp.maximum(signal_a, signal_b)
    return [
        (fa + fb) - fastest * (ub - ua)
        for fa, fb, ua, ub in zip(flux_a, flux_b, state_a, state_b)
    ]


def opening_kernel(
    rho_hbm, vel_hbm, pre_hbm, state_ref, zpay_ref, one_ref, two_ref, top_ref, rho_ref, vel_ref, pre_ref, sems
):
    planes, rows, width = rho_ref.shape
    pairs = ((rho_hbm, rho_ref), (vel_hbm, vel_ref), (pre_hbm, pre_ref))
    copies = [pltpu.make_async_copy(src, dst, sems.at[i]) for i, (src, dst) in enumerate(pairs)]
    for copy in copies:
        copy.start()
    for copy in copies:
        copy.wait()
    even = (lax.axis_index("group") & 1) == 0
    edge = list(range(REACH)) + list(range(planes - REACH, planes))
    fastest = None
    for z in range(planes):
        rho, p = rho_ref[z], pre_ref[z]
        v = [vel_ref[i, z] for i in range(3)]
        signal = jnp.abs(v[0]) + jnp.abs(v[1]) + jnp.abs(v[2]) + 3.0 * jnp.sqrt(HEAT_RATIO * p / rho)
        signal = jnp.max(signal.reshape(rows // SUB, SUB, width), axis=0)
        fastest = signal if fastest is None else jnp.maximum(fastest, signal)
        kinetic = 0.5 * rho * (v[0] * v[0] + v[1] * v[1] + v[2] * v[2])
        fields = [rho, rho * v[0], rho * v[1], rho * v[2], p / (HEAT_RATIO - 1.0) + kinetic]
        for f in range(5):
            state_ref[f, z] = fields[f]
            if z in edge:
                zpay_ref[f, edge.index(z)] = fields[f]
            at = (f * planes + z) * REACH
            low, high = fields[f][:REACH], fields[f][rows - REACH :]
            one_ref[at : at + REACH, :] = jnp.where(even, high, low)
            two_ref[at : at + REACH, :] = jnp.where(even, low, high)
    top_ref[...] = fastest
    for ref in (one_ref, two_ref):
        ref[5 * planes * REACH :, :] = fastest


def opening(density, velocity, pressure):
    planes, rows, width = density.shape
    f32 = jnp.float32
    return pl.pallas_call(
        opening_kernel,
        out_shape=[
            jax.ShapeDtypeStruct((5, planes, rows, width), f32),
            jax.ShapeDtypeStruct((5, 2 * REACH, rows, width), f32),
            jax.ShapeDtypeStruct((5 * planes * REACH + SUB, width), f32),
            jax.ShapeDtypeStruct((5 * planes * REACH + SUB, width), f32),
            jax.ShapeDtypeStruct((SUB, width), f32),
        ],
        in_specs=[pl.BlockSpec(memory_space=pltpu.HBM)] * 3,
        out_specs=[VMEM] * 5,
        scratch_shapes=[
            pltpu.VMEM(density.shape, f32),
            pltpu.VMEM(velocity.shape, f32),
            pltpu.VMEM(pressure.shape, f32),
            pltpu.SemaphoreType.DMA((3,)),
        ],
        name="opening",
        compiler_params=grant(8),
    )(*[pltpu.with_memory_space_constraint(a, pltpu.HBM) for a in (density, velocity, pressure)])


def window_kernel(
    state_ref, one_ref, two_ref, top_ref, wide_ref, first_ref, second_ref, peak_ref
):
    planes, rows, width = state_ref.shape[1:]
    sent = slice(5 * planes * REACH, 5 * planes * REACH + SUB)
    peak_ref[...] = jnp.maximum(top_ref[...], jnp.maximum(one_ref[sent, :], two_ref[sent, :]))
    total = wide_ref.shape[2]
    group, groups = lax.axis_index("group"), lax.axis_size("group")
    even, even_image = (group & 1) == 0, (lax.axis_index("image") & 1) == 0
    lane = lax.broadcasted_iota(jnp.int32, (SUB, width), 1)
    for f in range(5):
        sign = -1.0 if f == 1 else 1.0
        for z in range(planes):
            at = (f * planes + z) * REACH
            wide_ref[f, z, REACH : REACH + rows, :] = state_ref[f, z]
            mirrored = [state_ref[f, z, r : r + 1, :] * sign for r in range(REACH - 1, -1, -1)]
            one, two = one_ref[at : at + REACH, :], two_ref[at : at + REACH, :]
            below = jnp.where(
                group == 0, jnp.concatenate(mirrored, axis=0), jnp.where(even, two, one)
            )
            wide_ref[f, z, :REACH, :] = below
            mirrored = [state_ref[f, z, rows - 1 - r : rows - r, :] * sign for r in range(REACH)]
            above = jnp.where(
                group == groups - 1, jnp.concatenate(mirrored, axis=0), jnp.where(even, one, two)
            )
            wide_ref[f, z, REACH + rows : 2 * REACH + rows, :] = above

    def fields(f, carry):
        for t in range(total // SUB):
            cut = slice(SUB * t, SUB * (t + 1))
            right = jnp.zeros((SUB, width), jnp.float32)
            left = right
            for z in range(planes):
                start = WINDOW * (z + REACH)
                inside = (lane >= start) & (lane < start + WINDOW)
                values = wide_ref[f, z, cut, :]
                right = jnp.where(inside, turned(values, start - (width - 2 * REACH)), right)
                left = jnp.where(inside, turned(values, start - (width - REACH)), left)
            first_ref[f, cut, :] = jnp.where(even_image, left, right)
            second_ref[f, cut, :] = jnp.where(even_image, right, left)
        return carry

    lax.fori_loop(0, 5, fields, 0)


def windows(state, one, two, top):
    planes, rows, width = state.shape[1:]
    total = padded_rows(rows)
    f32 = jnp.float32
    return pl.pallas_call(
        window_kernel,
        out_shape=[
            jax.ShapeDtypeStruct((5, planes, total, width), f32),
            jax.ShapeDtypeStruct((5, total, width), f32),
            jax.ShapeDtypeStruct((5, total, width), f32),
            jax.ShapeDtypeStruct((SUB, width), f32),
        ],
        in_specs=[VMEM] * 4,
        out_specs=[VMEM] * 4,
        name="windows",
        compiler_params=grant(8),
    )(state, one, two, top)


def strip_kernel(wide_ref, first_ref, second_ref, got_first, got_second, strips_ref, pay_ref):
    even = (lax.axis_index("image") & 1) == 0
    planes, total, width = wide_ref.shape[1:]
    rows = total - 2 * REACH - (total - 2 * REACH) % SUB
    lane = lax.broadcasted_iota(jnp.int32, (SUB, width), 1)
    column = lane % WINDOW
    span = WINDOW * REACH
    start, last = WINDOW * REACH, WINDOW * planes
    far = WINDOW * (REACH + planes)
    for f in range(5):
        for t in range(total // SUB):
            cut = slice(SUB * t, SUB * (t + 1))
            first, second = first_ref[f, cut, :], second_ref[f, cut, :]
            near, after = got_first[f, cut, :], got_second[f, cut, :]
            right = jnp.where(
                column >= 2 * REACH, jnp.where(even, near, after), jnp.where(even, second, first)
            )
            left = jnp.where(
                column < REACH, jnp.where(even, after, near), jnp.where(even, first, second)
            )
            strips_ref[0, f, cut, :] = left
            strips_ref[1, f, cut, :] = right
            sent = jnp.where(lane < span, turned(right, -last), left)
            pay_ref[f, cut, :] = jnp.where(lane >= far, turned(right, far - start), sent)
        low, high = REACH - 1, REACH + rows
        for side, (near, next_one) in enumerate(((0, 1), (planes - 1, planes - 2))):
            at = total + SUB * side
            pay_ref[f, at : at + 2, :] = wide_ref[f, near, low - 1 : low + 1, :]
            pay_ref[f, at + 2 : at + 3, :] = wide_ref[f, next_one, low : low + 1, :]
            pay_ref[f, at + 3 : at + 5, :] = wide_ref[f, near, high : high + 2, :]
            pay_ref[f, at + 5 : at + 6, :] = wide_ref[f, next_one, high : high + 1, :]
            pay_ref[f, at + 6 : at + 8, :] = jnp.zeros((2, width), jnp.float32)


def strips_of(wide, first, second, got_first, got_second):
    _, total, width = wide.shape[1:]
    f32 = jnp.float32
    return pl.pallas_call(
        strip_kernel,
        out_shape=[
            jax.ShapeDtypeStruct((2, 5, total, width), f32),
            jax.ShapeDtypeStruct((5, total + 2 * SUB, width), f32),
        ],
        in_specs=[VMEM] * 5,
        out_specs=[VMEM] * 2,
        name="strips",
        compiler_params=grant(8),
    )(wide, first, second, got_first, got_second)


def blend(section, base, here, change, half):
    if section == 0:
        return here + half * change
    if section == 1:
        return 0.75 * base + 0.25 * (here + half * change)
    return base * (1.0 / 3.0) + (2.0 / 3.0) * (here + half * change)


def along_y(state, flux, pressure, signal):
    other = [ahead(v) for v in state]
    flux_other = fluxes(other, other[2] * (1.0 / other[0]), ahead(pressure), 2)
    g = face(flux, flux_other, state, other, signal, ahead(signal))
    return [behind(v) - v for v in g]


def section_kernel(shared, *refs):
    if shared:
        wide_ref, zone_ref, pay_ref, strips_ref, top_ref = refs[:5]
        zone_refs, pay_refs = (zone_ref, zone_ref), (pay_ref, pay_ref)
        rest = refs[5:]
    else:
        wide_ref, strips_ref, top_ref = refs[0], refs[5], refs[6]
        zone_refs, pay_refs = refs[1:3], refs[3:5]
        rest = refs[7:]
    out_ref, rho_ref, heat_ref = rest[:3]
    main, strip, (fx, gx, acc, fz, gz) = rest[3:7], rest[7:11], rest[11:16]
    strip_buffers = (rest[16:19], rest[19:22])
    planes, total, width = wide_ref.shape[1:]
    rows = out_ref.shape[2]
    tiles = total // SUB
    lane = lax.broadcasted_iota(jnp.int32, (SUB, width), 1)
    far = WINDOW * (REACH + planes)
    for f in range(5):
        for z in range(planes):
            main[0][f, z + REACH, :total, :] = wide_ref[f, z]
        for z in range(REACH):
            main[0][f, z, REACH : REACH + rows, :] = zone_refs[0][f, REACH + z]
            main[0][f, planes + REACH + z, REACH : REACH + rows, :] = zone_refs[1][f, z]
        low, high = REACH - 1, REACH + rows
        for pay, near, next_one, at in (
            (pay_refs[1], planes + REACH, planes + REACH + 1, total),
            (pay_refs[0], REACH - 1, REACH - 2, total + SUB),
        ):
            main[0][f, near, low - 1 : low + 1, :] = pay[f, at : at + 2, :]
            main[0][f, next_one, low : low + 1, :] = pay[f, at + 2 : at + 3, :]
            main[0][f, near, high : high + 2, :] = pay[f, at + 3 : at + 5, :]
            main[0][f, next_one, high : high + 1, :] = pay[f, at + 5 : at + 6, :]
        for t in range(tiles):
            cut = slice(SUB * t, SUB * (t + 1))
            before, after = pay_refs[0][f, cut, :], pay_refs[1][f, cut, :]
            span = WINDOW * REACH
            left = jnp.where(lane < span, turned(before, -WINDOW * planes), strips_ref[0, f, cut, :])
            strip[0][0, f, cut, :] = jnp.where(lane >= far, turned(after, far - span), left)
            right = jnp.where(lane < span, before, strips_ref[1, f, cut, :])
            strip[0][1, f, cut, :] = jnp.where(lane >= far, after, right)
    half = jnp.broadcast_to(0.5 * COURANT / jnp.max(top_ref[...], keepdims=True), (SUB, width))

    def x_pass(buffers, load, t):
        fx, gx, acc = buffers
        here, there = slice(SUB * t, SUB * (t + 1)), slice(SUB * t + 1, SUB * (t + 1) + 1)
        a, b = load(here), load(there)
        g = face(
            [fx[f, here, :] for f in range(5)],
            [fx[f, there, :] for f in range(5)],
            a,
            b,
            fx[5, here, :],
            fx[5, there, :],
        )
        for f in range(5):
            gx[f, SUB * (t + 1) : SUB * (t + 2), :] = g[f]
            below = gx[f, SUB * (t + 1) - 1 : SUB * (t + 2) - 1, :]
            acc[f, here, :] = acc[f, here, :] + (below - g[f])

    def keep_x(fx, state, ux, pressure, sound, cut):
        for f, v in enumerate(fluxes(state, ux, pressure, 1)):
            fx[f, cut, :] = v
        fx[5, cut, :] = jnp.abs(ux) + sound

    def strip_start(section, side, t):
        source, (fx, gx, acc) = strip[section], strip_buffers[side]
        cut = pl.ds(pl.multiple_of(SUB * t, SUB), SUB)
        state = [source[side, f, cut, :] for f in range(5)]
        ux, uy, uz, pressure, sound = primitives(*state)
        keep_x(fx, state, ux, pressure, sound, cut)
        change = along_y(state, fluxes(state, uy, pressure, 2), pressure, jnp.abs(uy) + sound)
        signal = jnp.abs(uz) + sound
        other = [ahead(v, WINDOW) for v in state]
        _, _, normal, pressure_other, sound_other = primitives(*other)
        g = face(
            fluxes(state, uz, pressure, 3),
            fluxes(other, normal, pressure_other, 3),
            state,
            other,
            signal,
            jnp.abs(normal) + sound_other,
        )
        for f in range(5):
            acc[f, cut, :] = change[f] + (behind(g[f], WINDOW) - g[f])

    def strip_finish(section, side):
        source, target, buffers = strip[section], strip[section + 1], strip_buffers[side]
        for t in range(tiles):
            cut = slice(SUB * t, SUB * (t + 1))
            x_pass(buffers, lambda at: [source[side, f, at, :] for f in range(5)], t)
            for f in range(5):
                here, base = source[side, f, cut, :], strip[0][side, f, cut, :]
                target[side, f, cut, :] = blend(section, base, here, buffers[2][f, cut, :], half)

    def main_section(section, first, last):
        source, target, base = main[section], main[section + 1], main[0]

        def plane(w, with_face, with_finish, with_sides):
            def load(cut):
                return [source[f, w, cut, :] for f in range(5)]

            for t in range(tiles):
                cut = slice(SUB * t, SUB * (t + 1))
                state = load(cut)
                ux, uy, uz, pressure, sound = primitives(*state)
                flux, signal = fluxes(state, uz, pressure, 3), jnp.abs(uz) + sound
                if with_face:
                    before = [source[f, w - 1, cut, :] for f in range(5)]
                    flux_before = [fz[f, cut, :] for f in range(5)]
                    g = face(flux_before, flux, before, state, fz[5, cut, :], signal)
                    for f in range(5):
                        if with_finish:
                            change = acc[f, cut, :] + (gz[f, cut, :] - g[f])
                            started = base[f, w - 1, cut, :] if section else None
                            target[f, w - 1, cut, :] = blend(section, started, before[f], change, half)
                        if with_sides:
                            gz[f, cut, :] = g[f]
                if with_sides or not with_face:
                    for f in range(5):
                        fz[f, cut, :] = flux[f]
                    fz[5, cut, :] = signal
                if with_sides:
                    keep_x(fx, state, ux, pressure, sound, cut)
                    flux = fluxes(state, uy, pressure, 2)
                    change = along_y(state, flux, pressure, jnp.abs(uy) + sound)
                    for f in range(5):
                        acc[f, cut, :] = change[f]
                    if t:
                        x_pass((fx, gx, acc), load, t - 1)
            if with_sides:
                x_pass((fx, gx, acc), load, tiles - 1)

        plane(first - 1, False, False, False)
        plane(first, True, False, True)

        count = last - first - 1
        for t in range(tiles - count):
            for side in range(2):
                strip_start(section, side, count + t)

        def step(with_strips):
            def one_plane(w, carry):
                plane(w, True, True, True)
                for side in range(2 if with_strips else 0):
                    strip_start(section, side, w - first - 1)
                return carry

            return one_plane

        middle = first + 1 + min(count, tiles)
        lax.fori_loop(first + 1, middle, step(True), 0)
        if middle < last:
            lax.fori_loop(middle, last, step(False), 0)
        plane(last, True, True, False)

    for section in range(3):
        main_section(section, 1 + section, planes + 2 * REACH - 1 - section)
        for side in range(2):
            strip_finish(section, side)
    column = lane % WINDOW
    for f in range(5):
        for t in range(rows // SUB):
            cut = slice(SUB * t + REACH, SUB * (t + 1) + REACH)
            edge = jnp.where(
                column < 2 * REACH, strip[3][1, f, cut, :], behind(strip[3][0, f, cut, :], REACH)
            )
            for z in range(planes):
                placed = turned(edge, width - REACH - (WINDOW * (z + REACH) + REACH))
                inner = main[3][f, z + REACH, cut, :]
                out_ref[f, z, SUB * t : SUB * (t + 1), :] = jnp.where(
                    (lane < REACH) | (lane >= width - REACH), placed, inner
                )
    for z in range(planes):
        state = [out_ref[f, z] for f in range(5)]
        rho_ref[z] = state[0]
        heat_ref[z] = primitives(*state)[3] / state[0]


def sections(wide, zones, pays, strips, top, rows):
    planes, total, width = wide.shape[1:]
    f32 = jnp.float32
    shared = len(zones) == 1
    tall, deep = total + SUB, planes + 2 * REACH
    args = [wide, *zones, *pays, strips, top]
    brick = jax.ShapeDtypeStruct((planes, rows, width), f32)
    return pl.pallas_call(
        functools.partial(section_kernel, shared),
        out_shape=[pltpu.VMEM((5, planes, rows, width), f32), brick, brick],
        in_specs=[VMEM] * len(args),
        out_specs=[VMEM] * 3,
        scratch_shapes=[pltpu.VMEM((5, deep, tall, width), f32)] * 4
        + [pltpu.VMEM((2, 5, tall, width), f32)] * 4
        + [
            pltpu.VMEM((6, tall, width), f32),
            pltpu.VMEM((5, tall, width), f32),
            pltpu.VMEM((5, total, width), f32),
            pltpu.VMEM((6, total, width), f32),
            pltpu.VMEM((5, total, width), f32),
        ]
        + [
            pltpu.VMEM((6, tall, width), f32),
            pltpu.VMEM((5, tall, width), f32),
            pltpu.VMEM((5, total, width), f32),
        ]
        * 2,
        name="sections",
        compiler_params=grant(24),
    )(*args)


def lanes(values, index):
    return lax.gather(
        values,
        index[..., None],
        lax.GatherDimensionNumbers(
            offset_dims=(),
            collapsed_slice_dims=(1,),
            start_index_map=(1,),
            operand_batching_dims=(0,),
            start_indices_batching_dims=(0,),
        ),
        slice_sizes=(1, 1),
        mode=lax.GatherScatterMode.PROMISE_IN_BOUNDS,
    )


LEVELS = 65535
UNROLL = 8


def render_kernel(
    scale, begin, count, halves, rho_ref, heat_ref, palette_ref, index_ref, *refs
):
    outs, (table, ke, ko, we, wo, thick) = refs[: len(refs) - 6], refs[len(refs) - 6 :]
    planes, _, width = rho_ref.shape
    count_tf, bins = index_ref.shape
    half = bins // 2
    chosen = index_ref[...]
    if halves:
        swapped = pltpu.roll(chosen, count_tf // 2, axis=0)
        chosen = jnp.where(lax.axis_index("depth") == 0, swapped, chosen)
    colours = palette_ref[...]
    least = jnp.min(colours, keepdims=True)
    step = jnp.maximum(jnp.max(colours, keepdims=True) - least, 1e-6) * (1.0 / LEVELS)
    coded = ((colours - least) / step + 0.5).astype(jnp.int32)
    words = [(coded[c : c + 1] - (LEVELS + 1) // 2) * (LEVELS + 1) + coded[c + 1 : c + 2] for c in (0, 2)]
    lane = lax.broadcasted_iota(jnp.int32, (count_tf, half), 1)
    low, high = chosen[:, :half], chosen[:, half:]
    for parity in range(2):
        at = lane * 2 + parity
        inside = jnp.where(at < half, at, at - half)
        colour = jnp.where(at < half, lanes(low, inside), lanes(high, inside))
        wrapped = jnp.where(colour < half, colour, colour - half)
        for pair in range(2):
            first = jnp.broadcast_to(words[pair][:, :half], (count_tf, half))
            second = jnp.broadcast_to(words[pair][:, half:], (count_tf, half))
            table[pair, parity] = jnp.where(
                colour < half, lanes(first, wrapped), lanes(second, wrapped)
            )
    step_wide = jnp.broadcast_to(step, (SUB, width))
    for z in range(planes):
        for t in range(count // SUB):
            cut, from_cut = slice(SUB * t, SUB * (t + 1)), slice(begin + SUB * t, begin + SUB * (t + 1))
            rho = rho_ref[z, from_cut, :]
            position = jnp.clip(rho - 0.5, 0.0, 1.0) * (bins - 1)
            cell = jnp.minimum(position.astype(jnp.int32), bins - 2)
            even = (cell + 1) >> 1
            odd = cell >> 1
            ke[z, cut, :] = even
            ko[z, cut, :] = odd
            we[z, cut, :] = (1.0 - jnp.abs(position - (2 * even).astype(jnp.float32))) * step_wide
            wo[z, cut, :] = (1.0 - jnp.abs(position - (2 * odd + 1).astype(jnp.float32))) * step_wide
            thick[z, cut, :] = rho * (-scale * math.log2(math.e))
    tables = [[table[pair, p] for p in range(2)] for pair in range(2)]
    base_low = jnp.broadcast_to(least, (count_tf, width))
    base_high = base_low + jnp.broadcast_to(step, (count_tf, width)) * ((LEVELS + 1) // 2)

    def rays(group, carry):
        for i in range(UNROLL):
            ray(group * UNROLL + i)
        return carry

    def ray(x):
        trans = jnp.ones((count_tf, width), jnp.float32)
        light = [jnp.zeros((count_tf, width), jnp.float32) for _ in range(3)]
        for z in range(planes):

            def wide(ref, at=x):
                return jnp.broadcast_to(ref[z, pl.ds(at, 1), :], (count_tf, width))

            ie, io, fe, fo = wide(ke), wide(ko), wide(we), wide(wo)
            looked = []
            for pair in range(2):
                even, odd = lanes(tables[pair][0], ie), lanes(tables[pair][1], io)
                looked.append(
                    base_high
                    + (even >> 16).astype(jnp.float32) * fe
                    + (odd >> 16).astype(jnp.float32) * fo
                )
                looked.append(
                    base_low
                    + (even & LEVELS).astype(jnp.float32) * fe
                    + (odd & LEVELS).astype(jnp.float32) * fo
                )
            passed = trans * jnp.exp2(looked[3] * wide(thick))
            weight = (trans - passed) * wide(heat_ref, x + begin)
            light = [light[c] + looked[c] * weight for c in range(3)]
            trans = passed
        per_out = count_tf // len(outs)
        for c, values in enumerate(light + [trans]):
            for i, out in enumerate(outs):
                out[pl.ds(c * count + x, per_out, stride=4 * count), :] = values[
                    per_out * i : per_out * (i + 1)
                ]

    lax.fori_loop(0, count // UNROLL, rays, 0)


def render(rho, heat, palette, index, scale, begin, count, halves):
    planes, _, width = rho.shape
    count_tf, bins = index.shape
    parts = 2 if halves else 1
    per_out = count_tf // parts
    shape = jax.ShapeDtypeStruct((per_out * 4 * count, width), jnp.float32)
    scratch = [pltpu.VMEM((planes, count, width), t) for t in (jnp.int32,) * 2 + (jnp.float32,) * 3]
    outs = pl.pallas_call(
        functools.partial(render_kernel, scale, begin, count, halves),
        out_shape=[shape] * parts,
        in_specs=[VMEM] * 4,
        out_specs=[VMEM] * parts,
        scratch_shapes=[pltpu.VMEM((2, 2, count_tf, bins // 2), jnp.int32)] + scratch,
        compiler_params=grant(8),
    )(rho, heat, palette, index)
    return [out.reshape(per_out, 4, count, width) for out in outs]


def exchange_max(value, axis, step):
    size = lax.axis_size(axis)
    if size & (size - 1) == 0:
        route = [(i, i ^ step) for i in range(size)]
    else:
        route = along(axis, step, True)
    return jnp.maximum(value, lax.ppermute(value, axis, route))


def last_rounds(value):
    images, depth = lax.axis_size("image"), lax.axis_size("depth")
    if images != 4 or depth != 2:
        return largest(largest(value, "image", 2), "depth")
    others = []
    for flip_depth, flip_image in ((1, 0), (0, 2), (1, 2)):
        route = [
            (d * images + i, (d ^ flip_depth) * images + (i ^ flip_image))
            for d in range(depth)
            for i in range(images)
        ]
        others.append(lax.ppermute(value, ("depth", "image"), route))
    for other in others:
        value = jnp.maximum(value, other)
    return value


def largest(value, axis, step=1):
    while step < lax.axis_size(axis):
        value = exchange_max(value, axis, step)
        step *= 2
    return value


def composed(shares):
    light, passed = None, None
    for d in range(shares.shape[0]):
        slab = shares[d]
        light = slab[:, :3] if d == 0 else light + passed * slab[:, :3]
        passed = slab[:, 3:] if d == 0 else passed * slab[:, 3:]
    return light


def along(axis, distance, wrap):
    size = lax.axis_size(axis)
    if wrap:
        return [(i, (i + distance) % size) for i in range(size)]
    return [(i, i + distance) for i in range(size) if 0 <= i + distance < size]


def paired(axis, start, wrap):
    size = lax.axis_size(axis)
    assert not wrap or size % 2 == 0, "odd ring"
    couples = [(i, (i + 1) % size) for i in range(start, size, 2) if wrap or i + 1 < size]
    return couples + [(j, i) for i, j in couples]


def pictured(rho, heat, palette, index):
    depth = lax.axis_size("depth")
    planes, rows, _ = rho.shape
    scale = 2.0 / (planes * depth)
    if depth != 2:
        (shares,) = render(rho, heat, palette, index, scale, 0, rows, False)
        parts = shares.reshape((depth, shares.shape[0] // depth) + shares.shape[1:])
        return composed(lax.all_to_all(parts, "depth", 0, 0, tiled=True))
    pieces = PIECES if rows % (PIECES * SUB) == 0 else 1
    chunk = rows // pieces
    kept, sent = [], []
    for i in range(pieces):
        other, own = render(rho, heat, palette, index, scale, i * chunk, chunk, True)
        kept.append(own)
        sent.append(lax.ppermute(other, "depth", along("depth", 1, True)))
    in_front = lax.axis_index("depth") == 0
    shown = []
    for own, other in zip(kept, sent):
        front, back = jnp.where(in_front, own, other), jnp.where(in_front, other, own)
        shown.append(front[:, :3] + front[:, 3:] * back[:, :3])
    return jnp.concatenate(shown, axis=2)


def whole_step(density, velocity, pressure, palette, palette_index):
    depth = lax.axis_size("depth")
    _, rows = density.shape[:2]
    state, zone, one, two, top = opening(density, velocity, pressure)

    def both_ways(block):
        if depth == 2:
            return (lax.ppermute(block, "depth", along("depth", 1, True)),)
        return tuple(lax.ppermute(block, "depth", along("depth", d, True)) for d in (1, -1))

    got_one = lax.ppermute(one, "group", paired("group", 0, False))
    got_two = lax.ppermute(two, "group", paired("group", 1, False))
    zones = both_ways(zone)
    wide, first, second, top = windows(state, got_one, got_two, top)
    got_first = lax.ppermute(first, "image", paired("image", 0, True))
    got_second = lax.ppermute(second, "image", paired("image", 1, True))
    if lax.axis_size("group") == 4:
        top = exchange_max(top, "group", 2)
    else:
        top = largest(top, "group")
    top = exchange_max(top, "image", 1)
    got_first, got_second, top = lax.optimization_barrier((got_first, got_second, top))
    strips, pay = strips_of(wide, first, second, got_first, got_second)
    pays = both_ways(pay)
    top = last_rounds(top)
    fluid_state, rho, heat = sections(wide, zones, pays, strips, top, rows)
    return (fluid_state, pictured(rho, heat, palette, palette_index))


def solution(mesh):
    return jax.shard_map(
        whole_step,
        mesh=mesh,
        in_specs=(
            P("depth", "group", "image"),
            P(None, "depth", "group", "image"),
            P("depth", "group", "image"),
            P(),
            P(),
        ),
        out_specs=(P(None, "depth", "group", "image"), P("depth", None, "group", "image")),
        check_vma=False,
    )
```

```python
import functools
import math

import jax
import jax.numpy as jnp
from jax import lax
from jax.experimental import pallas as pl
from jax.experimental.pallas import tpu as pltpu
from jax.sharding import PartitionSpec as P


HEAT_RATIO = 1.4
COURANT = 0.8
REACH = 3
WINDOW = 3 * REACH
SUB = 8
PIECES = 3
VMEM = pl.BlockSpec(memory_space=pltpu.VMEM)
MIB = 1 << 20


def grant(mib):
    return pltpu.CompilerParams(vmem_limit_bytes=mib * MIB)


def ahead(values, distance=1):
    return pltpu.roll(values, values.shape[-1] - distance, axis=values.ndim - 1)


def behind(values, distance=1):
    return pltpu.roll(values, distance, axis=values.ndim - 1)


def turned(values, shift):
    return pltpu.roll(values, shift % values.shape[-1], axis=values.ndim - 1)


def padded_rows(rows):
    return -(-(rows + 2 * REACH) // SUB) * SUB


def primitives(rho, mx, my, mz, energy):
    inverse = 1.0 / rho
    ux, uy, uz = mx * inverse, my * inverse, mz * inverse
    pressure = (HEAT_RATIO - 1.0) * (energy - 0.5 * (mx * ux + my * uy + mz * uz))
    sound = jnp.sqrt(HEAT_RATIO * pressure * inverse)
    return ux, uy, uz, pressure, sound


def fluxes(state, normal, pressure, component):
    _, mx, my, mz, energy = state
    rows = [state[component], mx * normal, my * normal, mz * normal, (energy + pressure) * normal]
    rows[component] = rows[component] + pressure
    return rows


def face(flux_a, flux_b, state_a, state_b, signal_a, signal_b):
    fastest = jnp.maximum(signal_a, signal_b)
    return [
        (fa + fb) - fastest * (ub - ua)
        for fa, fb, ua, ub in zip(flux_a, flux_b, state_a, state_b)
    ]


def opening_kernel(
    rho_hbm, vel_hbm, pre_hbm, state_ref, zpay_ref, one_ref, two_ref, top_ref, rho_ref, vel_ref, pre_ref, sems
):
    planes, rows, width = rho_ref.shape
    pairs = ((rho_hbm, rho_ref), (vel_hbm, vel_ref), (pre_hbm, pre_ref))
    copies = [pltpu.make_async_copy(src, dst, sems.at[i]) for i, (src, dst) in enumerate(pairs)]
    for copy in copies:
        copy.start()
    for copy in copies:
        copy.wait()
    even = (lax.axis_index("group") & 1) == 0
    edge = list(range(REACH)) + list(range(planes - REACH, planes))
    fastest = None
    for z in range(planes):
        rho, p = rho_ref[z], pre_ref[z]
        v = [vel_ref[i, z] for i in range(3)]
        signal = jnp.abs(v[0]) + jnp.abs(v[1]) + jnp.abs(v[2]) + 3.0 * jnp.sqrt(HEAT_RATIO * p / rho)
        signal = jnp.max(signal.reshape(rows // SUB, SUB, width), axis=0)
        fastest = signal if fastest is None else jnp.maximum(fastest, signal)
        kinetic = 0.5 * rho * (v[0] * v[0] + v[1] * v[1] + v[2] * v[2])
        fields = [rho, rho * v[0], rho * v[1], rho * v[2], p / (HEAT_RATIO - 1.0) + kinetic]
        for f in range(5):
            state_ref[f, z] = fields[f]
            if z in edge:
                zpay_ref[f, edge.index(z)] = fields[f]
            at = (f * planes + z) * REACH
            low, high = fields[f][:REACH], fields[f][rows - REACH :]
            one_ref[at : at + REACH, :] = jnp.where(even, high, low)
            two_ref[at : at + REACH, :] = jnp.where(even, low, high)
    top_ref[...] = fastest
    for ref in (one_ref, two_ref):
        ref[5 * planes * REACH :, :] = fastest


def opening(density, velocity, pressure):
    planes, rows, width = density.shape
    f32 = jnp.float32
    return pl.pallas_call(
        opening_kernel,
        out_shape=[
            jax.ShapeDtypeStruct((5, planes, rows, width), f32),
            jax.ShapeDtypeStruct((5, 2 * REACH, rows, width), f32),
            jax.ShapeDtypeStruct((5 * planes * REACH + SUB, width), f32),
            jax.ShapeDtypeStruct((5 * planes * REACH + SUB, width), f32),
            jax.ShapeDtypeStruct((SUB, width), f32),
        ],
        in_specs=[pl.BlockSpec(memory_space=pltpu.HBM)] * 3,
        out_specs=[VMEM] * 5,
        scratch_shapes=[
            pltpu.VMEM(density.shape, f32),
            pltpu.VMEM(velocity.shape, f32),
            pltpu.VMEM(pressure.shape, f32),
            pltpu.SemaphoreType.DMA((3,)),
        ],
        name="opening",
        compiler_params=grant(8),
    )(*[pltpu.with_memory_space_constraint(a, pltpu.HBM) for a in (density, velocity, pressure)])


def window_kernel(
    state_ref, one_ref, two_ref, top_ref, wide_ref, first_ref, second_ref, peak_ref
):
    planes, rows, width = state_ref.shape[1:]
    sent = slice(5 * planes * REACH, 5 * planes * REACH + SUB)
    peak_ref[...] = jnp.maximum(top_ref[...], jnp.maximum(one_ref[sent, :], two_ref[sent, :]))
    total = wide_ref.shape[2]
    group, groups = lax.axis_index("group"), lax.axis_size("group")
    even, even_image = (group & 1) == 0, (lax.axis_index("image") & 1) == 0
    lane = lax.broadcasted_iota(jnp.int32, (SUB, width), 1)
    for f in range(5):
        sign = -1.0 if f == 1 else 1.0
        for z in range(planes):
            at = (f * planes + z) * REACH
            wide_ref[f, z, REACH : REACH + rows, :] = state_ref[f, z]
            mirrored = [state_ref[f, z, r : r + 1, :] * sign for r in range(REACH - 1, -1, -1)]
            one, two = one_ref[at : at + REACH, :], two_ref[at : at + REACH, :]
            below = jnp.where(
                group == 0, jnp.concatenate(mirrored, axis=0), jnp.where(even, two, one)
            )
            wide_ref[f, z, :REACH, :] = below
            mirrored = [state_ref[f, z, rows - 1 - r : rows - r, :] * sign for r in range(REACH)]
            above = jnp.where(
                group == groups - 1, jnp.concatenate(mirrored, axis=0), jnp.where(even, one, two)
            )
            wide_ref[f, z, REACH + rows : 2 * REACH + rows, :] = above

    def fields(f, carry):
        for t in range(total // SUB):
            cut = slice(SUB * t, SUB * (t + 1))
            right = jnp.zeros((SUB, width), jnp.float32)
            left = right
            for z in range(planes):
                start = WINDOW * (z + REACH)
                inside = (lane >= start) & (lane < start + WINDOW)
                values = wide_ref[f, z, cut, :]
                right = jnp.where(inside, turned(values, start - (width - 2 * REACH)), right)
                left = jnp.where(inside, turned(values, start - (width - REACH)), left)
            first_ref[f, cut, :] = jnp.where(even_image, left, right)
            second_ref[f, cut, :] = jnp.where(even_image, right, left)
        return carry

    lax.fori_loop(0, 5, fields, 0)


def windows(state, one, two, top):
    planes, rows, width = state.shape[1:]
    total = padded_rows(rows)
    f32 = jnp.float32
    return pl.pallas_call(
        window_kernel,
        out_shape=[
            jax.ShapeDtypeStruct((5, planes, total, width), f32),
            jax.ShapeDtypeStruct((5, total, width), f32),
            jax.ShapeDtypeStruct((5, total, width), f32),
            jax.ShapeDtypeStruct((SUB, width), f32),
        ],
        in_specs=[VMEM] * 4,
        out_specs=[VMEM] * 4,
        name="windows",
        compiler_params=grant(8),
    )(state, one, two, top)


def strip_kernel(wide_ref, first_ref, second_ref, got_first, got_second, strips_ref, pay_ref):
    even = (lax.axis_index("image") & 1) == 0
    planes, total, width = wide_ref.shape[1:]
    rows = total - 2 * REACH - (total - 2 * REACH) % SUB
    lane = lax.broadcasted_iota(jnp.int32, (SUB, width), 1)
    column = lane % WINDOW
    span = WINDOW * REACH
    start, last = WINDOW * REACH, WINDOW * planes
    far = WINDOW * (REACH + planes)
    for f in range(5):
        for t in range(total // SUB):
            cut = slice(SUB * t, SUB * (t + 1))
            first, second = first_ref[f, cut, :], second_ref[f, cut, :]
            near, after = got_first[f, cut, :], got_second[f, cut, :]
            right = jnp.where(
                column >= 2 * REACH, jnp.where(even, near, after), jnp.where(even, second, first)
            )
            left = jnp.where(
                column < REACH, jnp.where(even, after, near), jnp.where(even, first, second)
            )
            strips_ref[0, f, cut, :] = left
            strips_ref[1, f, cut, :] = right
            sent = jnp.where(lane < span, turned(right, -last), left)
            pay_ref[f, cut, :] = jnp.where(lane >= far, turned(right, far - start), sent)
        low, high = REACH - 1, REACH + rows
        for side, (near, next_one) in enumerate(((0, 1), (planes - 1, planes - 2))):
            at = total + SUB * side
            pay_ref[f, at : at + 2, :] = wide_ref[f, near, low - 1 : low + 1, :]
            pay_ref[f, at + 2 : at + 3, :] = wide_ref[f, next_one, low : low + 1, :]
            pay_ref[f, at + 3 : at + 5, :] = wide_ref[f, near, high : high + 2, :]
            pay_ref[f, at + 5 : at + 6, :] = wide_ref[f, next_one, high : high + 1, :]
            pay_ref[f, at + 6 : at + 8, :] = jnp.zeros((2, width), jnp.float32)


def strips_of(wide, first, second, got_first, got_second):
    _, total, width = wide.shape[1:]
    f32 = jnp.float32
    return pl.pallas_call(
        strip_kernel,
        out_shape=[
            jax.ShapeDtypeStruct((2, 5, total, width), f32),
            jax.ShapeDtypeStruct((5, total + 2 * SUB, width), f32),
        ],
        in_specs=[VMEM] * 5,
        out_specs=[VMEM] * 2,
        name="strips",
        compiler_params=grant(8),
    )(wide, first, second, got_first, got_second)


def blend(section, base, here, change, half):
    if section == 0:
        return here + half * change
    if section == 1:
        return 0.75 * base + 0.25 * (here + half * change)
    return base * (1.0 / 3.0) + (2.0 / 3.0) * (here + half * change)


def along_y(state, flux, pressure, signal, anew=False):
    other = [ahead(v) for v in state]
    if anew:
        _, normal, _, pressure, sound = primitives(*other)
        g = face(
            flux, fluxes(other, normal, pressure, 2), state, other, signal, jnp.abs(normal) + sound
        )
        return [behind(v) - v for v in g]
    flux_other = fluxes(other, other[2] * (1.0 / other[0]), ahead(pressure), 2)
    g = face(flux, flux_other, state, other, signal, ahead(signal))
    return [behind(v) - v for v in g]


def section_kernel(shared, *refs):
    if shared:
        wide_ref, zone_ref, pay_ref, strips_ref, top_ref = refs[:5]
        zone_refs, pay_refs = (zone_ref, zone_ref), (pay_ref, pay_ref)
        rest = refs[5:]
    else:
        wide_ref, strips_ref, top_ref = refs[0], refs[5], refs[6]
        zone_refs, pay_refs = refs[1:3], refs[3:5]
        rest = refs[7:]
    out_ref, rho_ref, heat_ref = rest[:3]
    main, strip, (fx, gx, acc, fz, gz) = rest[3:7], rest[7:11], rest[11:16]
    strip_buffers = (rest[16:19], rest[19:22])
    planes, total, width = wide_ref.shape[1:]
    rows = out_ref.shape[2]
    tiles = total // SUB
    lane = lax.broadcasted_iota(jnp.int32, (SUB, width), 1)
    far = WINDOW * (REACH + planes)
    for f in range(5):
        for z in range(planes):
            main[0][f, z + REACH, :total, :] = wide_ref[f, z]
        for z in range(REACH):
            main[0][f, z, REACH : REACH + rows, :] = zone_refs[0][f, REACH + z]
            main[0][f, planes + REACH + z, REACH : REACH + rows, :] = zone_refs[1][f, z]
        low, high = REACH - 1, REACH + rows
        for pay, near, next_one, at in (
            (pay_refs[1], planes + REACH, planes + REACH + 1, total),
            (pay_refs[0], REACH - 1, REACH - 2, total + SUB),
        ):
            main[0][f, near, low - 1 : low + 1, :] = pay[f, at : at + 2, :]
            main[0][f, next_one, low : low + 1, :] = pay[f, at + 2 : at + 3, :]
            main[0][f, near, high : high + 2, :] = pay[f, at + 3 : at + 5, :]
            main[0][f, next_one, high : high + 1, :] = pay[f, at + 5 : at + 6, :]
        for t in range(tiles):
            cut = slice(SUB * t, SUB * (t + 1))
            before, after = pay_refs[0][f, cut, :], pay_refs[1][f, cut, :]
            span = WINDOW * REACH
            left = jnp.where(lane < span, turned(before, -WINDOW * planes), strips_ref[0, f, cut, :])
            strip[0][0, f, cut, :] = jnp.where(lane >= far, turned(after, far - span), left)
            right = jnp.where(lane < span, before, strips_ref[1, f, cut, :])
            strip[0][1, f, cut, :] = jnp.where(lane >= far, after, right)
    half = jnp.broadcast_to(0.5 * COURANT / jnp.max(top_ref[...], keepdims=True), (SUB, width))

    def x_pass(buffers, load, t):
        fx, gx, acc = buffers
        here, there = slice(SUB * t, SUB * (t + 1)), slice(SUB * t + 1, SUB * (t + 1) + 1)
        a, b = load(here), load(there)
        g = face(
            [fx[f, here, :] for f in range(5)],
            [fx[f, there, :] for f in range(5)],
            a,
            b,
            fx[5, here, :],
            fx[5, there, :],
        )
        for f in range(5):
            gx[f, SUB * (t + 1) : SUB * (t + 2), :] = g[f]
            below = gx[f, SUB * (t + 1) - 1 : SUB * (t + 2) - 1, :]
            acc[f, here, :] = acc[f, here, :] + (below - g[f])

    def keep_x(fx, state, ux, pressure, sound, cut):
        for f, v in enumerate(fluxes(state, ux, pressure, 1)):
            fx[f, cut, :] = v
        fx[5, cut, :] = jnp.abs(ux) + sound

    def strip_start(section, side, t):
        source, (fx, gx, acc) = strip[section], strip_buffers[side]
        cut = pl.ds(pl.multiple_of(SUB * t, SUB), SUB)
        state = [source[side, f, cut, :] for f in range(5)]
        ux, uy, uz, pressure, sound = primitives(*state)
        keep_x(fx, state, ux, pressure, sound, cut)
        flux_y, signal_y = fluxes(state, uy, pressure, 2), jnp.abs(uy) + sound
        change = along_y(state, flux_y, pressure, signal_y, True)
        signal = jnp.abs(uz) + sound
        other = [ahead(v, WINDOW) for v in state]
        _, _, normal, pressure_other, sound_other = primitives(*other)
        g = face(
            fluxes(state, uz, pressure, 3),
            fluxes(other, normal, pressure_other, 3),
            state,
            other,
            signal,
            jnp.abs(normal) + sound_other,
        )
        for f in range(5):
            acc[f, cut, :] = change[f] + (behind(g[f], WINDOW) - g[f])

    def strip_finish(section, side):
        source, target, buffers = strip[section], strip[section + 1], strip_buffers[side]
        for t in range(tiles):
            cut = slice(SUB * t, SUB * (t + 1))
            x_pass(buffers, lambda at: [source[side, f, at, :] for f in range(5)], t)
            for f in range(5):
                here, base = source[side, f, cut, :], strip[0][side, f, cut, :]
                target[side, f, cut, :] = blend(section, base, here, buffers[2][f, cut, :], half)

    def main_section(section, first, last):
        source, target, base = main[section], main[section + 1], main[0]

        def plane(w, with_face, with_finish, with_sides):
            def load(cut):
                return [source[f, w, cut, :] for f in range(5)]

            for t in range(tiles):
                cut = slice(SUB * t, SUB * (t + 1))
                state = load(cut)
                ux, uy, uz, pressure, sound = primitives(*state)
                flux, signal = fluxes(state, uz, pressure, 3), jnp.abs(uz) + sound
                if with_face:
                    before = [source[f, w - 1, cut, :] for f in range(5)]
                    flux_before = [fz[f, cut, :] for f in range(5)]
                    g = face(flux_before, flux, before, state, fz[5, cut, :], signal)
                    for f in range(5):
                        if with_finish:
                            change = acc[f, cut, :] + (gz[f, cut, :] - g[f])
                            started = base[f, w - 1, cut, :] if section else None
                            target[f, w - 1, cut, :] = blend(section, started, before[f], change, half)
                        if with_sides:
                            gz[f, cut, :] = g[f]
                if with_sides or not with_face:
                    for f in range(5):
                        fz[f, cut, :] = flux[f]
                    fz[5, cut, :] = signal
                if with_sides:
                    keep_x(fx, state, ux, pressure, sound, cut)
                    flux = fluxes(state, uy, pressure, 2)
                    change = along_y(state, flux, pressure, jnp.abs(uy) + sound)
                    for f in range(5):
                        acc[f, cut, :] = change[f]
                    if t:
                        x_pass((fx, gx, acc), load, t - 1)
            if with_sides:
                x_pass((fx, gx, acc), load, tiles - 1)

        plane(first - 1, False, False, False)
        plane(first, True, False, True)

        count = last - first - 1
        for t in range(tiles - count):
            for side in range(2):
                strip_start(section, side, count + t)

        def step(with_strips):
            def one_plane(w, carry):
                plane(w, True, True, True)
                for side in range(2 if with_strips else 0):
                    strip_start(section, side, w - first - 1)
                return carry

            return one_plane

        middle = first + 1 + min(count, tiles)
        lax.fori_loop(first + 1, middle, step(True), 0)
        if middle < last:
            lax.fori_loop(middle, last, step(False), 0)
        plane(last, True, True, False)

    for section in range(3):
        main_section(section, 1 + section, planes + 2 * REACH - 1 - section)
        for side in range(2):
            strip_finish(section, side)
    column = lane % WINDOW
    for f in range(5):
        for t in range(rows // SUB):
            cut = slice(SUB * t + REACH, SUB * (t + 1) + REACH)
            edge = jnp.where(
                column < 2 * REACH, strip[3][1, f, cut, :], behind(strip[3][0, f, cut, :], REACH)
            )
            for z in range(planes):
                placed = turned(edge, width - REACH - (WINDOW * (z + REACH) + REACH))
                inner = main[3][f, z + REACH, cut, :]
                out_ref[f, z, SUB * t : SUB * (t + 1), :] = jnp.where(
                    (lane < REACH) | (lane >= width - REACH), placed, inner
                )
    for z in range(planes):
        state = [out_ref[f, z] for f in range(5)]
        rho_ref[z] = state[0]
        heat_ref[z] = primitives(*state)[3] / state[0]


def sections(wide, zones, pays, strips, top, rows):
    planes, total, width = wide.shape[1:]
    f32 = jnp.float32
    shared = len(zones) == 1
    tall, deep = total + SUB, planes + 2 * REACH
    args = [wide, *zones, *pays, strips, top]
    brick = jax.ShapeDtypeStruct((planes, rows, width), f32)
    return pl.pallas_call(
        functools.partial(section_kernel, shared),
        out_shape=[pltpu.VMEM((5, planes, rows, width), f32), brick, brick],
        in_specs=[VMEM] * len(args),
        out_specs=[VMEM] * 3,
        scratch_shapes=[pltpu.VMEM((5, deep, tall, width), f32)] * 4
        + [pltpu.VMEM((2, 5, tall, width), f32)] * 4
        + [
            pltpu.VMEM((6, tall, width), f32),
            pltpu.VMEM((5, tall, width), f32),
            pltpu.VMEM((5, total, width), f32),
            pltpu.VMEM((6, total, width), f32),
            pltpu.VMEM((5, total, width), f32),
        ]
        + [
            pltpu.VMEM((6, tall, width), f32),
            pltpu.VMEM((5, tall, width), f32),
            pltpu.VMEM((5, total, width), f32),
        ]
        * 2,
        name="sections",
        compiler_params=grant(24),
    )(*args)


def lanes(values, index):
    return lax.gather(
        values,
        index[..., None],
        lax.GatherDimensionNumbers(
            offset_dims=(),
            collapsed_slice_dims=(1,),
            start_index_map=(1,),
            operand_batching_dims=(0,),
            start_indices_batching_dims=(0,),
        ),
        slice_sizes=(1, 1),
        mode=lax.GatherScatterMode.PROMISE_IN_BOUNDS,
    )


LEVELS = 65535
UNROLL = 8


def render_kernel(
    scale, begin, count, halves, rho_ref, heat_ref, palette_ref, index_ref, *refs
):
    outs, (table, ke, ko, we, wo, thick) = refs[: len(refs) - 6], refs[len(refs) - 6 :]
    planes, _, width = rho_ref.shape
    count_tf, bins = index_ref.shape
    half = bins // 2
    chosen = index_ref[...]
    if halves:
        swapped = pltpu.roll(chosen, count_tf // 2, axis=0)
        chosen = jnp.where(lax.axis_index("depth") == 0, swapped, chosen)
    colours = palette_ref[...]
    least = jnp.min(colours, keepdims=True)
    step = jnp.maximum(jnp.max(colours, keepdims=True) - least, 1e-6) * (1.0 / LEVELS)
    coded = ((colours - least) / step + 0.5).astype(jnp.int32)
    words = [(coded[c : c + 1] - (LEVELS + 1) // 2) * (LEVELS + 1) + coded[c + 1 : c + 2] for c in (0, 2)]
    lane = lax.broadcasted_iota(jnp.int32, (count_tf, half), 1)
    low, high = chosen[:, :half], chosen[:, half:]
    for parity in range(2):
        at = lane * 2 + parity
        inside = jnp.where(at < half, at, at - half)
        colour = jnp.where(at < half, lanes(low, inside), lanes(high, inside))
        wrapped = jnp.where(colour < half, colour, colour - half)
        for pair in range(2):
            first = jnp.broadcast_to(words[pair][:, :half], (count_tf, half))
            second = jnp.broadcast_to(words[pair][:, half:], (count_tf, half))
            table[pair, parity] = jnp.where(
                colour < half, lanes(first, wrapped), lanes(second, wrapped)
            )
    step_wide = jnp.broadcast_to(step, (SUB, width))
    for z in range(planes):
        for t in range(count // SUB):
            cut, from_cut = slice(SUB * t, SUB * (t + 1)), slice(begin + SUB * t, begin + SUB * (t + 1))
            rho = rho_ref[z, from_cut, :]
            position = jnp.clip(rho - 0.5, 0.0, 1.0) * (bins - 1)
            cell = jnp.minimum(position.astype(jnp.int32), bins - 2)
            even = (cell + 1) >> 1
            odd = cell >> 1
            ke[z, cut, :] = even
            ko[z, cut, :] = odd
            we[z, cut, :] = (1.0 - jnp.abs(position - (2 * even).astype(jnp.float32))) * step_wide
            wo[z, cut, :] = (1.0 - jnp.abs(position - (2 * odd + 1).astype(jnp.float32))) * step_wide
            thick[z, cut, :] = rho * (-scale * math.log2(math.e))
    tables = [[table[pair, p] for p in range(2)] for pair in range(2)]
    base_low = jnp.broadcast_to(least, (count_tf, width))
    base_high = base_low + jnp.broadcast_to(step, (count_tf, width)) * ((LEVELS + 1) // 2)

    def rays(group, carry):
        for i in range(UNROLL):
            ray(group * UNROLL + i)
        return carry

    def ray(x):
        trans = jnp.ones((count_tf, width), jnp.float32)
        light = [jnp.zeros((count_tf, width), jnp.float32) for _ in range(3)]
        for z in range(planes):

            def wide(ref, at=x):
                return jnp.broadcast_to(ref[z, pl.ds(at, 1), :], (count_tf, width))

            ie, io, fe, fo = wide(ke), wide(ko), wide(we), wide(wo)
            looked = []
            for pair in range(2):
                even, odd = lanes(tables[pair][0], ie), lanes(tables[pair][1], io)
                looked.append(
                    base_high
                    + (even >> 16).astype(jnp.float32) * fe
                    + (odd >> 16).astype(jnp.float32) * fo
                )
                looked.append(
                    base_low
                    + (even & LEVELS).astype(jnp.float32) * fe
                    + (odd & LEVELS).astype(jnp.float32) * fo
                )
            passed = trans * jnp.exp2(looked[3] * wide(thick))
            weight = (trans - passed) * wide(heat_ref, x + begin)
            light = [light[c] + looked[c] * weight for c in range(3)]
            trans = passed
        per_out = count_tf // len(outs)
        for c, values in enumerate(light + [trans]):
            for i, out in enumerate(outs):
                out[pl.ds(c * count + x, per_out, stride=4 * count), :] = values[
                    per_out * i : per_out * (i + 1)
                ]

    lax.fori_loop(0, count // UNROLL, rays, 0)


def render(rho, heat, palette, index, scale, begin, count, halves):
    planes, _, width = rho.shape
    count_tf, bins = index.shape
    parts = 2 if halves else 1
    per_out = count_tf // parts
    shape = jax.ShapeDtypeStruct((per_out * 4 * count, width), jnp.float32)
    scratch = [pltpu.VMEM((planes, count, width), t) for t in (jnp.int32,) * 2 + (jnp.float32,) * 3]
    outs = pl.pallas_call(
        functools.partial(render_kernel, scale, begin, count, halves),
        out_shape=[shape] * parts,
        in_specs=[VMEM] * 4,
        out_specs=[VMEM] * parts,
        scratch_shapes=[pltpu.VMEM((2, 2, count_tf, bins // 2), jnp.int32)] + scratch,
        compiler_params=grant(8),
    )(rho, heat, palette, index)
    return [out.reshape(per_out, 4, count, width) for out in outs]


def exchange_max(value, axis, step):
    size = lax.axis_size(axis)
    if size & (size - 1) == 0:
        route = [(i, i ^ step) for i in range(size)]
    else:
        route = along(axis, step, True)
    return jnp.maximum(value, lax.ppermute(value, axis, route))


def last_rounds(value):
    images, depth = lax.axis_size("image"), lax.axis_size("depth")
    if images != 4 or depth != 2:
        return largest(largest(value, "image", 2), "depth")
    others = []
    for flip_depth, flip_image in ((1, 0), (0, 2), (1, 2)):
        route = [
            (d * images + i, (d ^ flip_depth) * images + (i ^ flip_image))
            for d in range(depth)
            for i in range(images)
        ]
        others.append(lax.ppermute(value, ("depth", "image"), route))
    for other in others:
        value = jnp.maximum(value, other)
    return value


def largest(value, axis, step=1):
    while step < lax.axis_size(axis):
        value = exchange_max(value, axis, step)
        step *= 2
    return value


def composed(shares):
    light, passed = None, None
    for d in range(shares.shape[0]):
        slab = shares[d]
        light = slab[:, :3] if d == 0 else light + passed * slab[:, :3]
        passed = slab[:, 3:] if d == 0 else passed * slab[:, 3:]
    return light


def along(axis, distance, wrap):
    size = lax.axis_size(axis)
    if wrap:
        return [(i, (i + distance) % size) for i in range(size)]
    return [(i, i + distance) for i in range(size) if 0 <= i + distance < size]


def paired(axis, start, wrap):
    size = lax.axis_size(axis)
    assert not wrap or size % 2 == 0, "odd ring"
    couples = [(i, (i + 1) % size) for i in range(start, size, 2) if wrap or i + 1 < size]
    return couples + [(j, i) for i, j in couples]


def pictured(rho, heat, palette, index):
    depth = lax.axis_size("depth")
    planes, rows, _ = rho.shape
    scale = 2.0 / (planes * depth)
    if depth != 2:
        (shares,) = render(rho, heat, palette, index, scale, 0, rows, False)
        parts = shares.reshape((depth, shares.shape[0] // depth) + shares.shape[1:])
        return composed(lax.all_to_all(parts, "depth", 0, 0, tiled=True))
    pieces = PIECES if rows % (PIECES * SUB) == 0 else 1
    chunk = rows // pieces
    kept, sent = [], []
    for i in range(pieces):
        other, own = render(rho, heat, palette, index, scale, i * chunk, chunk, True)
        kept.append(own)
        sent.append(lax.ppermute(other, "depth", along("depth", 1, True)))
    in_front = lax.axis_index("depth") == 0
    shown = []
    for own, other in zip(kept, sent):
        front, back = jnp.where(in_front, own, other), jnp.where(in_front, other, own)
        shown.append(front[:, :3] + front[:, 3:] * back[:, :3])
    return jnp.concatenate(shown, axis=2)


def whole_step(density, velocity, pressure, palette, palette_index):
    depth = lax.axis_size("depth")
    _, rows = density.shape[:2]
    state, zone, one, two, top = opening(density, velocity, pressure)

    def both_ways(block):
        if depth == 2:
            return (lax.ppermute(block, "depth", along("depth", 1, True)),)
        return tuple(lax.ppermute(block, "depth", along("depth", d, True)) for d in (1, -1))

    got_one = lax.ppermute(one, "group", paired("group", 0, False))
    got_two = lax.ppermute(two, "group", paired("group", 1, False))
    zones = both_ways(zone)
    wide, first, second, top = windows(state, got_one, got_two, top)
    got_first = lax.ppermute(first, "image", paired("image", 0, True))
    got_second = lax.ppermute(second, "image", paired("image", 1, True))
    if lax.axis_size("group") == 4:
        top = exchange_max(top, "group", 2)
    else:
        top = largest(top, "group")
    top = exchange_max(top, "image", 1)
    got_first, got_second, top = lax.optimization_barrier((got_first, got_second, top))
    strips, pay = strips_of(wide, first, second, got_first, got_second)
    pays = both_ways(pay)
    top = last_rounds(top)
    fluid_state, rho, heat = sections(wide, zones, pays, strips, top, rows)
    return (fluid_state, pictured(rho, heat, palette, palette_index))


def solution(mesh):
    return jax.shard_map(
        whole_step,
        mesh=mesh,
        in_specs=(
            P("depth", "group", "image"),
            P(None, "depth", "group", "image"),
            P("depth", "group", "image"),
            P(),
            P(),
        ),
        out_specs=(P(None, "depth", "group", "image"), P("depth", None, "group", "image")),
        check_vma=False,
    )
```
